32 devices in a mesh: ping: 4 (over z), band: 8 (over y, x, core).
Axes of the slice: x: 2, y: 2, z: 4, core: 2. Of those that a mesh axis runs over, the one named last changes fastest.
Arguments:
- staves: bfloat16 [2, 64, 256, 8, 512], P(None, 'ping', 'band'), may hold values from -6 to 6
- weights: bfloat16 [2, 256, 512, 512], P(None, 'band'), may hold values from -0.25 to 0.25
- replica: float32 [2, 2048], replicated, may hold values from -5 to 5
- start: int32 [64, 512], P('ping', 'band'), may hold values from 0 to 1535
- length: int32 [64, 512], P('ping', 'band'), may hold values from 64 to 512
Outputs:
- centroid: float32 [64, 512], P('ping', 'band')
- energy: float32 [64, 512], P('ping', 'band')
The draws below stay inside these ranges and needn't reach their ends.
Inputs may be any that keep to these rules, and one draw needn't show every extreme that they name: Every window lies inside the beam's samples: start + length <= 2048.
All inputs are finite; a program needn't handle non-finite values.
Results may differ from the reference program's by a relative error of at most 0.0004.
Values may be sent and summed in bfloat16 or wider, within the bound.
No kernel may reach another device: no remote copies, remote signals or barrier semaphores. Data moves between devices by JAX's collectives and lax.ppermute only.
A program may use at most 192 MiB of HBM per device.

```python
import math
import jax
import jax.numpy as jnp
from jax import lax

STAVES = 512
BEAMS = 512
BANDS = 256
BINS = 8
LENGTH = 2048
PINGS = 64


def touch_ends(drawn, rng, least, high):
    longest = drawn.shape.index(max(drawn.shape))
    spots = []
    for shift in (0, 1):
        where = [jax.random.randint(jax.random.fold_in(rng, axis), (), 0, length) for axis, length in enumerate(drawn.shape)]
        where[longest] = (where[longest] + shift) % drawn.shape[longest]
        spots.append(tuple(where))
    return drawn.at[spots[0]].set(least).at[spots[1]].set(high)


def block_levels(rng, shape, shards, least, largest):
    loudness, own = 1.0, jax.random.fold_in(rng, 6)
    for dim, parts in shards:
        heights = jnp.exp(jax.random.uniform(jax.random.fold_in(own, dim), (parts,), jnp.float32, least / len(shards), largest / len(shards)))
        loudness = loudness * jnp.repeat(heights, shape[dim] // parts).reshape([-1 if axis == dim else 1 for axis in range(len(shape))])
    return loudness


def gaussian(key, shape, spread, reach, split=(), kind=jnp.bfloat16):
    values = spread * jax.random.normal(key, shape, jnp.float32)
    if split:
        values = values * block_levels(key, shape, split, -0.22, 0.18)
    return jnp.clip(values, -reach, reach).astype(kind)


def setup_inputs(seed: int = 0) -> dict:
    seeds = jax.random.split(jax.random.key(seed), 6)
    staves = gaussian(seeds[0], (2, PINGS, BANDS, BINS, STAVES), 1.0, 6.0, ((1, 4), (2, 8)))
    weights = gaussian(seeds[1], (2, BANDS, STAVES, BEAMS), STAVES ** -0.5, 0.25, ((1, 8),))
    replica = gaussian(seeds[2], (2, LENGTH), 1.0, 5.0, (), jnp.float32)
    start = touch_ends(jax.random.randint(seeds[3], (PINGS, BEAMS), 0, LENGTH - LENGTH // 4), jax.random.fold_in(seeds[3], 1), 0, (LENGTH - LENGTH // 4) - 1).astype(jnp.int32)
    length = touch_ends(jax.random.randint(seeds[4], (PINGS, BEAMS), LENGTH // 32, LENGTH // 4 + 1), jax.random.fold_in(seeds[4], 1), LENGTH // 32, (LENGTH // 4 + 1) - 1).astype(jnp.int32)
    return {"staves": staves, "weights": weights, "replica": replica, "start": start, "length": length}


TAPS = (1.0, 2.0, 3.0, 4.0, 5.0, 4.0, 3.0, 2.0, 1.0)


def dft_tables(length_total):
    freqs = jnp.arange(length_total, dtype=jnp.int32)
    phases = (freqs[:, None] * freqs[None, :]) % length_total
    angles = phases.astype(jnp.float32) * (2.0 * math.pi / length_total)
    return jnp.cos(angles).astype(jnp.bfloat16), jnp.sin(angles).astype(jnp.bfloat16)


def envelope_rows(spec_re, spec_im, replica, cos_table, sin_table):
    comp_re = (spec_re * replica[0] + spec_im * replica[1]).astype(jnp.bfloat16)
    comp_im = (spec_im * replica[0] - spec_re * replica[1]).astype(jnp.bfloat16)
    wave_re = jnp.dot(comp_re, cos_table, preferred_element_type=jnp.float32) - jnp.dot(comp_im, sin_table, preferred_element_type=jnp.float32)
    wave_im = jnp.dot(comp_re, sin_table, preferred_element_type=jnp.float32) + jnp.dot(comp_im, cos_table, preferred_element_type=jnp.float32)
    return (wave_re * wave_re + wave_im * wave_im) * (1.0 / (16.0 * cos_table.shape[0]))


def beamform_band(operands):
    stave_band, weight_band = operands
    flat_re = stave_band[0].reshape(-1, stave_band.shape[-1])
    flat_im = stave_band[1].reshape(-1, stave_band.shape[-1])
    beam_re = jnp.dot(flat_re, weight_band[0], preferred_element_type=jnp.float32) - jnp.dot(flat_im, weight_band[1], preferred_element_type=jnp.float32)
    beam_im = jnp.dot(flat_re, weight_band[1], preferred_element_type=jnp.float32) + jnp.dot(flat_im, weight_band[0], preferred_element_type=jnp.float32)
    stacked = jnp.stack([beam_re, beam_im]).astype(jnp.bfloat16)
    return stacked.reshape(2, stave_band.shape[1], stave_band.shape[2], weight_band.shape[-1])


def smooth_pings(padded, first_ping, total_pings, ping_count):
    positions = first_ping + jnp.arange(ping_count + 8, dtype=jnp.int32) - 4
    inside = ((positions >= 0) & (positions < total_pings)).astype(jnp.float32)
    summed = jnp.zeros(padded.shape[:0] + (ping_count,) + padded.shape[1:], jnp.float32)
    weight_sum = jnp.zeros((ping_count,), jnp.float32)
    for offset in range(9):
        summed = summed + TAPS[offset] * padded[offset:offset + ping_count]
        weight_sum = weight_sum + TAPS[offset] * inside[offset:offset + ping_count]
    return summed / weight_sum[:, None, None]


def window_stats(smoothed, start, length):
    samples = jnp.arange(smoothed.shape[-1], dtype=jnp.int32)
    window_start = start[..., None]
    finish = (start + length)[..., None]
    inside = (samples >= window_start) & (samples < finish)
    offsets = samples.astype(jnp.float32) - start.astype(jnp.float32)[..., None] + 0.5
    energy_total = jnp.sum(jnp.where(inside, smoothed, 0.0), axis=-1)
    moment = jnp.sum(jnp.where(inside, smoothed * offsets, 0.0), axis=-1)
    widths = length.astype(jnp.float32)
    return moment / (widths * (energy_total + 1e-6)), energy_total / widths


def reference(staves, weights, replica, start, length):
    beams = lax.map(beamform_band, (jnp.moveaxis(staves, 2, 0), jnp.moveaxis(weights, 1, 0)))
    spectra = jnp.transpose(beams, (1, 2, 4, 0, 3)).reshape(2, PINGS, BEAMS, LENGTH)
    cos_table, sin_table = dft_tables(LENGTH)

    def per_ping(spectrum):
        return envelope_rows(spectrum[0].astype(jnp.float32), spectrum[1].astype(jnp.float32), replica, cos_table, sin_table)

    envelope = lax.map(per_ping, jnp.moveaxis(spectra, 1, 0))
    padded = jnp.pad(envelope, ((4, 4), (0, 0), (0, 0)))
    smoothed = smooth_pings(padded, 0, PINGS, PINGS)
    centroid, energy = window_stats(smoothed, start, length)
    return (centroid, energy)
```

```python
import functools
import math

import jax
import jax.numpy as jnp
from jax import lax
from jax.experimental import pallas as pl
from jax.experimental.pallas import tpu as pltpu
from jax.sharding import PartitionSpec as P


TAPS = (1.0, 2.0, 3.0, 4.0, 5.0, 4.0, 3.0, 2.0, 1.0)
REACH = len(TAPS) // 2
LANES = 128
PAIR = 2
HEAD_STEPS = 4
STEP_BANDS = 2


def extended(array, sides, width):
    for axis, dim in sides:
        count, length = (lax.axis_size(axis), array.shape[dim])
        up = [(i, (i + 1) % count) for i in range(count - 1)]
        down = [(j, i) for i, j in up]
        last = lax.slice_in_dim(array, length - width, length, axis=dim)
        initial = lax.slice_in_dim(array, 0, width, axis=dim)
        before = lax.ppermute(last, axis, up)
        after = lax.ppermute(initial, axis, down)
        array = jnp.concatenate([before, array, after], axis=dim)
    return array


def dft_tables(length_total):
    freqs = jnp.arange(length_total, dtype=jnp.int32)
    phases = freqs[:, None] * freqs[None, :] % length_total
    angles = phases.astype(jnp.float32) * (2.0 * math.pi / length_total)
    return (jnp.cos(angles).astype(jnp.bfloat16), jnp.sin(angles).astype(jnp.bfloat16))


def envelope_rows(spec_re, spec_im, replica, cos_table, sin_table):
    comp_re = (spec_re * replica[0] + spec_im * replica[1]).astype(jnp.bfloat16)
    comp_im = (spec_im * replica[0] - spec_re * replica[1]).astype(jnp.bfloat16)
    wave_re = jnp.dot(comp_re, cos_table, preferred_element_type=jnp.float32) - jnp.dot(
        comp_im, sin_table, preferred_element_type=jnp.float32
    )
    wave_im = jnp.dot(comp_re, sin_table, preferred_element_type=jnp.float32) + jnp.dot(
        comp_im, cos_table, preferred_element_type=jnp.float32
    )
    return (wave_re * wave_re + wave_im * wave_im) * (1.0 / (16.0 * cos_table.shape[0]))


def tap_weights(first_ping, total_pings, ping_count):
    positions = first_ping + jnp.arange(ping_count + 2 * REACH, dtype=jnp.int32) - REACH
    inside = ((positions >= 0) & (positions < total_pings)).astype(jnp.float32)
    weight_sum = jnp.zeros((ping_count,), jnp.float32)
    for offset, tap in enumerate(TAPS):
        weight_sum = weight_sum + tap * inside[offset : offset + ping_count]
    return weight_sum


def smooth_pings(padded, first_ping, total_pings, ping_count):
    summed = jnp.zeros((ping_count,) + padded.shape[1:], jnp.float32)
    for offset, tap in enumerate(TAPS):
        summed = summed + tap * padded[offset : offset + ping_count]
    return summed / tap_weights(first_ping, total_pings, ping_count)[:, None, None]


def window_stats(smoothed, start, length):
    samples = jnp.arange(smoothed.shape[-1], dtype=jnp.int32)
    window_start = start[..., None]
    finish = (start + length)[..., None]
    inside = (samples >= window_start) & (samples < finish)
    offsets = samples.astype(jnp.float32) - start.astype(jnp.float32)[..., None] + 0.5
    energy_total = jnp.sum(jnp.where(inside, smoothed, 0.0), axis=-1)
    moment = jnp.sum(jnp.where(inside, smoothed * offsets, 0.0), axis=-1)
    widths = length.astype(jnp.float32)
    return (moment / (widths * (energy_total + 1e-06)), energy_total / widths)


def local_plain(staves, weights, replica, start, length):
    ping_index = lax.axis_index("ping")
    ping_total = lax.axis_size("ping")
    beam_re = jnp.einsum(
        "pkfs,ksb->kpfb", staves[0], weights[0], preferred_element_type=jnp.float32
    ) - jnp.einsum("pkfs,ksb->kpfb", staves[1], weights[1], preferred_element_type=jnp.float32)
    beam_im = jnp.einsum(
        "pkfs,ksb->kpfb", staves[0], weights[1], preferred_element_type=jnp.float32
    ) + jnp.einsum("pkfs,ksb->kpfb", staves[1], weights[0], preferred_element_type=jnp.float32)
    beams = jnp.stack([beam_re, beam_im]).astype(jnp.bfloat16)
    cos_table, sin_table = dft_tables(replica.shape[1])
    turned = lax.all_to_all(beams, "band", split_axis=4, concat_axis=1, tiled=True)
    pings_here = turned.shape[2]
    beams_here = turned.shape[4]
    flat_rows = jnp.transpose(turned, (0, 2, 4, 1, 3)).reshape(2, pings_here * beams_here, -1)
    energy_rows = envelope_rows(
        flat_rows[0].astype(jnp.float32),
        flat_rows[1].astype(jnp.float32),
        replica,
        cos_table,
        sin_table,
    )
    envelope = energy_rows.reshape(pings_here, beams_here, -1)
    ping_count = envelope.shape[0]
    padded = extended(envelope.astype(jnp.bfloat16), (("ping", 0),), REACH).astype(envelope.dtype)
    smoothed = smooth_pings(padded, ping_index * ping_count, ping_total * ping_count, ping_count)
    centroid, energy = window_stats(smoothed, start, length)
    return (centroid, energy)


def beam_kernel(me_ref, x_ref, w_ref, rep_ref, *refs, count, first_band, splits):
    outs, stage = refs[:-1], refs[-1]
    bands = x_ref.shape[2]
    pings, bins, staves = x_ref.shape[1], x_ref.shape[3], x_ref.shape[4]
    rows = pings * bins
    half = pings // PAIR
    beams = w_ref.shape[3]
    span = 2 * LANES
    base = (first_band + pl.program_id(0) * bands) * bins
    q_rows = lax.broadcasted_iota(jnp.int32, (bins, rep_ref.shape[1]), 0)
    q_cols = lax.broadcasted_iota(jnp.int32, (bins, rep_ref.shape[1]), 1)

    def spectra(k):
        def part(which):
            flat = x_ref[which, :, k].astype(jnp.float32).reshape(rows, staves)
            return flat.astype(jnp.bfloat16)

        both = jnp.concatenate([part(0), part(1)], axis=0)
        mine = q_cols == q_rows + (base + k * bins)
        rep = [
            jnp.sum(jnp.where(mine, rep_ref[i : i + 1, :], 0.0), axis=1, keepdims=True)
            for i in range(2)
        ]
        return both, rep

    def compressed(k, both, rep, lo):
        by_re = jnp.dot(both, w_ref[0, k, :, lo : lo + span], preferred_element_type=jnp.float32)
        by_im = jnp.dot(both, w_ref[1, k, :, lo : lo + span], preferred_element_type=jnp.float32)
        beam_re = (by_re[:rows] - by_im[rows:]).astype(jnp.bfloat16).astype(jnp.float32)
        beam_im = (by_im[:rows] + by_re[rows:]).astype(jnp.bfloat16).astype(jnp.float32)
        beam_re = beam_re.reshape(pings, bins, span)
        beam_im = beam_im.reshape(pings, bins, span)
        return (beam_re * rep[0] + beam_im * rep[1], beam_im * rep[0] - beam_re * rep[1])

    for k in range(0, bands, 2):
        pair = [spectra(k), spectra(k + 1)]
        for lo in range(0, beams, span):
            done = [compressed(k + i, *pair[i], lo) for i in range(2)]
            for which in range(2):
                joined = jnp.concatenate([done[0][which], done[1][which]], axis=1)
                joined = joined.astype(jnp.bfloat16)
                for part in range(span // LANES):
                    lane = slice(part * LANES, (part + 1) * LANES)
                    owner = PAIR * (lo // LANES + part)
                    for slot in range(half):
                        to = slice(k * bins, (k + 2) * bins)
                        stage[owner, which, slot, to] = joined[slot, :, lane]
                        stage[owner + 1, which, slot, to] = joined[pings - 1 - slot, :, lane]
    for r in range(count):
        owner = lax.rem(me_ref[0] + r, count)
        slot = 0
        for i, size in enumerate(splits):
            outs[i * count + r][...] = stage[owner, :, slot : slot + size]
            slot += size


def beamform(me, staves, weights, replica, count, first_band, steps, bands, splits):
    pings, bins = staves.shape[1], staves.shape[3]
    depth, beams = weights.shape[2], weights.shape[3]
    local_q = weights.shape[1] * bins
    skip = first_band // bands
    rows = bands * bins
    shapes = [
        jax.ShapeDtypeStruct((2, size, steps * rows, LANES), jnp.bfloat16)
        for size in splits
        for _ in range(count)
    ]
    flops = 8 * steps * bands * pings * bins * depth * beams
    moved = 4 * steps * bands * depth * beams + 8 * steps * bands * pings * bins * depth
    return pl.pallas_call(
        functools.partial(beam_kernel, count=count, first_band=first_band, splits=splits),
        grid_spec=pltpu.PrefetchScalarGridSpec(
            num_scalar_prefetch=1,
            grid=(steps,),
            in_specs=[
                pl.BlockSpec((2, pings, bands, bins, depth), lambda s, me: (0, 0, skip + s, 0, 0)),
                pl.BlockSpec((2, bands, depth, beams), lambda s, me: (0, skip + s, 0, 0)),
                pl.BlockSpec((2, local_q), lambda s, me: (0, me[0])),
            ],
            out_specs=[
                pl.BlockSpec((2, shape.shape[1], rows, LANES), lambda s, me: (0, 0, s, 0))
                for shape in shapes
            ],
            scratch_shapes=[pltpu.VMEM((count, 2, pings // PAIR, rows, LANES), jnp.bfloat16)],
        ),
        out_shape=shapes,
        compiler_params=pltpu.CompilerParams(vmem_limit_bytes=48 << 20),
        cost_estimate=pl.CostEstimate(flops=flops, bytes_accessed=moved, transcendentals=0),
        name="beamform",
    )(me, staves, weights, replica)


def add(a, b):
    return (a[0] + b[0], a[1] + b[1])


def sub(a, b):
    return (a[0] - b[0], a[1] - b[1])


def turn_by(z, step, count):
    if step == 0:
        return z
    if 4 * step == count:
        return (z[1], -z[0])
    if 8 * step == count:
        scale = math.sqrt(0.5)
        return ((z[0] + z[1]) * scale, (z[1] - z[0]) * scale)
    if 8 * step == 3 * count:
        scale = math.sqrt(0.5)
        return ((z[1] - z[0]) * scale, (z[0] + z[1]) * -scale)
    angle = 2.0 * math.pi * step / count
    c, s = math.cos(angle), math.sin(angle)
    return (z[0] * c + z[1] * s, z[1] * c - z[0] * s)


def small_dft(values):
    count = len(values)
    if count == 1:
        return values
    middle = count // 2
    even = small_dft([add(values[i], values[i + middle]) for i in range(middle)])
    odd = small_dft(
        [turn_by(sub(values[i], values[i + middle]), i, count) for i in range(middle)]
    )
    return [even[i // 2] if i % 2 == 0 else odd[i // 2] for i in range(count)]


def turned_kernel(*refs, count, width):
    heads, tails = refs[:count], refs[count : 2 * count]
    table_ref, window_ref, out_ref, spec, power, acc = refs[2 * count :]
    step = pl.program_id(0)
    slots = 2
    head_rows, tail_rows = heads[0].shape[2], tails[0].shape[2]
    depth = head_rows + tail_rows
    block = 16

    def transform(sources, slot, row, to):
        values = [
            tuple(ref[i, slot, pl.ds(row, block), :].astype(jnp.float32) for i in range(2))
            for ref in sources
        ]
        lanes = slice(slot * LANES, (slot + 1) * LANES)
        for m, z in enumerate(small_dft(values)):
            spec[m, pl.ds(to, block), lanes] = z[0].astype(jnp.bfloat16)
            spec[m, pl.ds(depth + to, block), lanes] = z[1].astype(jnp.bfloat16)

    @pl.when(step == 0)
    def _():
        acc[...] = jnp.zeros_like(acc)
        for slot in range(slots):

            @pl.loop(0, head_rows // block)
            def _(i):
                row = pl.multiple_of(i * block, block)
                transform(heads, slot, row, row)

            @pl.loop(0, tail_rows // block)
            def _(i):
                row = pl.multiple_of(i * block, block)
                transform(tails, slot, row, pl.multiple_of(head_rows + row, block))

    wave = jnp.dot(table_ref[0], spec[step], preferred_element_type=jnp.float32)
    power[...] = wave[:depth] * wave[:depth] + wave[depth:] * wave[depth:]

    sub_row = lax.broadcasted_iota(jnp.int32, (8, LANES), 0)
    within = (count * sub_row + step).astype(jnp.float32)
    middles = [within - window_ref[0, o : o + 1, :] for o in range(width)]
    halves = [jnp.broadcast_to(window_ref[1, o : o + 1, :], (8, LANES)) for o in range(width)]
    totals = [acc[0, o] for o in range(width)]
    moments = [acc[1, o] for o in range(width)]

    def body(i, carry):
        totals, moments = list(carry[0]), list(carry[1])
        row = pl.multiple_of(i * 8, 8)
        one = power[pl.ds(row, 8), :LANES]
        two = power[pl.ds(row, 8), LANES:]
        both = one + two
        rising, falling = [one], [two]
        for _ in range(REACH):
            rising.append(rising[-1] + both)
            falling.append(falling[-1] + both)
        smoothed = rising + falling[::-1]
        sample = (i * (8 * count)).astype(jnp.float32)
        for o in range(width):
            offset = middles[o] + sample
            kept = jnp.where(jnp.abs(offset) < halves[o], smoothed[o], 0.0)
            totals[o] = totals[o] + kept
            moments[o] = moments[o] + kept * offset
        return tuple(totals), tuple(moments)

    totals, moments = lax.fori_loop(
        0, depth // 8, body, (tuple(totals), tuple(moments)), unroll=2
    )
    for o in range(width):
        acc[0, o] = totals[o]
        acc[1, o] = moments[o]

    @pl.when(step == count - 1)
    def _():
        out_ref[...] = jnp.sum(acc[...], axis=2)


def window_sums(heads, tails, table, windows, chunk):
    count = len(heads)
    width = 2 * REACH + 2
    head_rows, tail_rows = heads[0].shape[2], tails[0].shape[2]
    depth = head_rows + tail_rows
    flops = 2 * count * (2 * depth) * (2 * depth) * (2 * LANES)
    moved = 2 * table.size + 16 * count * depth * LANES
    return pl.pallas_call(
        functools.partial(turned_kernel, count=count, width=width),
        grid=(count,),
        in_specs=[
            pl.BlockSpec((2, 2, head_rows, LANES), lambda s: (0, chunk, 0, 0))
            for _ in range(count)
        ]
        + [pl.BlockSpec((2, 2, tail_rows, LANES), lambda s: (0, 0, 0, 0)) for _ in range(count)]
        + [
            pl.BlockSpec((1, 2 * depth, 2 * depth), lambda s: (s, 0, 0)),
            pl.BlockSpec((2, width, LANES), lambda s: (0, 0, 0)),
        ],
        out_specs=pl.BlockSpec((2, width, LANES), lambda s: (0, 0, 0)),
        out_shape=jax.ShapeDtypeStruct((2, width, LANES), jnp.float32),
        scratch_shapes=[
            pltpu.VMEM((count, 2 * depth, 2 * LANES), jnp.bfloat16),
            pltpu.VMEM((depth, 2 * LANES), jnp.float32),
            pltpu.VMEM((2, width, 8, LANES), jnp.float32),
        ],
        compiler_params=pltpu.CompilerParams(vmem_limit_bytes=32 << 20),
        cost_estimate=pl.CostEstimate(flops=flops, bytes_accessed=moved, transcendentals=0),
        name="window_sums",
    )(*heads, *tails, table, windows)


def wave_tables(count, depth):
    total = count * depth
    index = jnp.arange(depth, dtype=jnp.int32)
    angle = ((index[:, None] * index[None, :]) % depth).astype(jnp.float32) * (2.0 * math.pi / depth)
    turn = (jnp.arange(count, dtype=jnp.int32)[:, None] * index[None, :]).astype(jnp.float32)
    turn = turn * (2.0 * math.pi / total)
    small = (jnp.cos(angle), jnp.sin(angle), jnp.cos(turn), jnp.sin(turn))
    cos_a, sin_a, cos_b, sin_b = lax.optimization_barrier(small)
    cos_b, sin_b = cos_b[:, None, :], sin_b[:, None, :]
    cos = (cos_a * cos_b - sin_a * sin_b).astype(jnp.bfloat16)
    sin = (sin_a * cos_b + cos_a * sin_b).astype(jnp.bfloat16)
    upper = jnp.concatenate([cos, -sin], axis=2)
    lower = jnp.concatenate([sin, cos], axis=2)
    return jnp.concatenate([upper, lower], axis=1)


def local_fast(staves, weights, replica, start, length):
    count = lax.axis_size("band")
    blocks = lax.axis_size("ping")
    me = lax.axis_index("band")
    block = lax.axis_index("ping")
    second = lax.rem(me, PAIR) == 1
    pings, bands, bins = staves.shape[1:4]
    half = pings // PAIR
    chunks = half // 2
    depth = bands * bins
    mine = start.shape[1]

    def send(array, r):
        return lax.ppermute(array, "band", [(i, (i + r) % count) for i in range(count)])

    def partner(array):
        return lax.ppermute(array, "band", [(i, i ^ 1) for i in range(count)])

    def across(array, cross, second_up):
        pairs = []
        for b in range(blocks):
            for i in range(count):
                to = b + 1 if (i % PAIR == 1) == second_up else b - 1
                if 0 <= to < blocks:
                    pairs.append((b * count + i, to * count + (i ^ 1 if cross else i)))
        return lax.ppermute(array, ("ping", "band"), pairs)

    def framed(array, axis):
        return jnp.where(second, jnp.flip(array, axis), array)

    def halves_of(array):
        low, high = array[..., :mine], array[..., mine:]
        return jnp.where(second, high, low), jnp.where(second, low, high)

    def side_by_side(own, other):
        return jnp.where(
            second,
            jnp.concatenate([other, own], axis=-1),
            jnp.concatenate([own, other], axis=-1),
        )

    me_array = jnp.reshape(me, (1,)).astype(jnp.int32)
    head_bands = HEAD_STEPS * STEP_BANDS
    heads = beamform(me_array, staves, weights, replica, count, 0, HEAD_STEPS, STEP_BANDS, (half,))
    got_heads = [heads[0]] + [send(heads[r], r) for r in range(1, count)]

    rest = (bands - head_bands) // (2 * STEP_BANDS)
    tails = beamform(
        me_array, staves, weights, replica, count, head_bands, rest, 2 * STEP_BANDS, (2,) * chunks
    )
    got_tails = []
    for i in range(chunks):
        own = tails[i * count : (i + 1) * count]
        got_tails.append([own[0]] + [send(own[r], r) for r in range(1, count)])

    own_start, own_length, _ = lax.optimization_barrier((start, length, heads[0]))
    own = framed(jnp.stack([own_start, own_length]), 1)
    other = jnp.flip(partner(own), 1)
    near = side_by_side(own, other)[:, : half + REACH]
    same = across(own[:, pings - REACH :], False, False)
    cross = across(jnp.flip(own[:, :REACH], 1), True, True)
    spans = jnp.concatenate([side_by_side(same, cross), near], axis=1).astype(jnp.float32)
    windows = jnp.stack([spans[0] + (spans[1] - 1.0) * 0.5, spans[1] * 0.5])

    table = wave_tables(count, depth)

    width = 2 * REACH + 2
    reached = half + 2 * REACH
    sums = jnp.zeros((2, reached, LANES), jnp.float32)
    for i in range(chunks):
        part = window_sums(
            got_heads, got_tails[i], table, windows[:, 2 * i : 2 * i + width], i
        )
        sums = sums + jnp.pad(part, ((0, 0), (2 * i, reached - width - 2 * i), (0, 0)))
        if 2 * (i + 1) == REACH:
            edge_own, edge_other = halves_of(sums[:, :REACH])
            edge_same = across(edge_own, False, True)
            edge_cross = across(edge_other, True, True)

    kept, passed = halves_of(sums[:, REACH:])
    passed = partner(passed)

    def placed(array, before):
        after = pings - before - array.shape[1]
        return jnp.pad(array, ((0, 0), (before, after), (0, 0)))

    whole = placed(kept, 0) + placed(jnp.flip(passed, 1), pings - passed.shape[1])
    whole = whole + placed(edge_same, pings - REACH) + placed(jnp.flip(edge_cross, 1), 0)
    whole = framed(whole, 1)

    weight_sum = tap_weights(block * pings, blocks * pings, pings)
    scale = (1.0 / (16.0 * count * depth)) / weight_sum
    widths = length.astype(jnp.float32)
    energy_total = whole[0] * scale[:, None]
    moment = (whole[1] + whole[0] * (widths * 0.5)) * scale[:, None]
    return (moment / (widths * (energy_total + 1e-06)), energy_total / widths)


def fits(mesh, staves, weights):
    count, blocks = mesh.shape["band"], mesh.shape["ping"]
    pings, bands, bins, depth = staves.shape[1] // blocks, staves.shape[2] // count, *staves.shape[3:]
    beams = weights.shape[3]
    half = pings // PAIR
    return (
        count == 8
        and beams * PAIR == LANES * count
        and beams % (2 * LANES) == 0
        and pings % (2 * PAIR) == 0
        and half >= 2 * REACH
        and bins == 8
        and depth % LANES == 0
        and bands * bins % LANES == 0
        and bands > HEAD_STEPS * STEP_BANDS
        and (bands - HEAD_STEPS * STEP_BANDS) % (2 * STEP_BANDS) == 0
        and HEAD_STEPS * STEP_BANDS % (2 * STEP_BANDS) == 0
    )


def solution(mesh):
    in_specs = (
        P(None, "ping", "band", None, None),
        P(None, "band", None, None),
        P(),
        P("ping", "band"),
        P("ping", "band"),
    )
    out_specs = (P("ping", "band"), P("ping", "band"))

    def run(staves, weights, replica, start, length):
        local = local_fast if fits(mesh, staves, weights) else local_plain
        body = jax.shard_map(
            local, mesh=mesh, in_specs=in_specs, out_specs=out_specs, check_vma=False
        )
        return body(staves, weights, replica, start, length)

    return run
```

```python
import functools
import math

import jax
import jax.numpy as jnp
from jax import lax
from jax.experimental import pallas as pl
from jax.experimental.pallas import tpu as pltpu
from jax.sharding import PartitionSpec as P


TAPS = (1.0, 2.0, 3.0, 4.0, 5.0, 4.0, 3.0, 2.0, 1.0)
REACH = len(TAPS) // 2
LANES = 128
PAIR = 2
BLOCK = 16
HEAD_STEPS = 4
STEP_BANDS = 2


def extended(array, sides, width):
    for axis, dim in sides:
        count, length = (lax.axis_size(axis), array.shape[dim])
        up = [(i, (i + 1) % count) for i in range(count - 1)]
        down = [(j, i) for i, j in up]
        last = lax.slice_in_dim(array, length - width, length, axis=dim)
        initial = lax.slice_in_dim(array, 0, width, axis=dim)
        before = lax.ppermute(last, axis, up)
        after = lax.ppermute(initial, axis, down)
        array = jnp.concatenate([before, array, after], axis=dim)
    return array


def dft_tables(length_total):
    freqs = jnp.arange(length_total, dtype=jnp.int32)
    phases = freqs[:, None] * freqs[None, :] % length_total
    angles = phases.astype(jnp.float32) * (2.0 * math.pi / length_total)
    return (jnp.cos(angles).astype(jnp.bfloat16), jnp.sin(angles).astype(jnp.bfloat16))


def envelope_rows(spec_re, spec_im, replica, cos_table, sin_table):
    comp_re = (spec_re * replica[0] + spec_im * replica[1]).astype(jnp.bfloat16)
    comp_im = (spec_im * replica[0] - spec_re * replica[1]).astype(jnp.bfloat16)
    wave_re = jnp.dot(comp_re, cos_table, preferred_element_type=jnp.float32) - jnp.dot(
        comp_im, sin_table, preferred_element_type=jnp.float32
    )
    wave_im = jnp.dot(comp_re, sin_table, preferred_element_type=jnp.float32) + jnp.dot(
        comp_im, cos_table, preferred_element_type=jnp.float32
    )
    return (wave_re * wave_re + wave_im * wave_im) * (1.0 / (16.0 * cos_table.shape[0]))


def tap_weights(first_ping, total_pings, ping_count):
    positions = first_ping + jnp.arange(ping_count + 2 * REACH, dtype=jnp.int32) - REACH
    inside = ((positions >= 0) & (positions < total_pings)).astype(jnp.float32)
    weight_sum = jnp.zeros((ping_count,), jnp.float32)
    for offset, tap in enumerate(TAPS):
        weight_sum = weight_sum + tap * inside[offset : offset + ping_count]
    return weight_sum


def smooth_pings(padded, first_ping, total_pings, ping_count):
    summed = jnp.zeros((ping_count,) + padded.shape[1:], jnp.float32)
    for offset, tap in enumerate(TAPS):
        summed = summed + tap * padded[offset : offset + ping_count]
    return summed / tap_weights(first_ping, total_pings, ping_count)[:, None, None]


def window_stats(smoothed, start, length):
    samples = jnp.arange(smoothed.shape[-1], dtype=jnp.int32)
    window_start = start[..., None]
    finish = (start + length)[..., None]
    inside = (samples >= window_start) & (samples < finish)
    offsets = samples.astype(jnp.float32) - start.astype(jnp.float32)[..., None] + 0.5
    energy_total = jnp.sum(jnp.where(inside, smoothed, 0.0), axis=-1)
    moment = jnp.sum(jnp.where(inside, smoothed * offsets, 0.0), axis=-1)
    widths = length.astype(jnp.float32)
    return (moment / (widths * (energy_total + 1e-06)), energy_total / widths)


def local_plain(staves, weights, replica, start, length):
    ping_index = lax.axis_index("ping")
    ping_total = lax.axis_size("ping")
    beam_re = jnp.einsum(
        "pkfs,ksb->kpfb", staves[0], weights[0], preferred_element_type=jnp.float32
    ) - jnp.einsum("pkfs,ksb->kpfb", staves[1], weights[1], preferred_element_type=jnp.float32)
    beam_im = jnp.einsum(
        "pkfs,ksb->kpfb", staves[0], weights[1], preferred_element_type=jnp.float32
    ) + jnp.einsum("pkfs,ksb->kpfb", staves[1], weights[0], preferred_element_type=jnp.float32)
    beams = jnp.stack([beam_re, beam_im]).astype(jnp.bfloat16)
    cos_table, sin_table = dft_tables(replica.shape[1])
    turned = lax.all_to_all(beams, "band", split_axis=4, concat_axis=1, tiled=True)
    pings_here = turned.shape[2]
    beams_here = turned.shape[4]
    flat_rows = jnp.transpose(turned, (0, 2, 4, 1, 3)).reshape(2, pings_here * beams_here, -1)
    energy_rows = envelope_rows(
        flat_rows[0].astype(jnp.float32),
        flat_rows[1].astype(jnp.float32),
        replica,
        cos_table,
        sin_table,
    )
    envelope = energy_rows.reshape(pings_here, beams_here, -1)
    ping_count = envelope.shape[0]
    padded = extended(envelope.astype(jnp.bfloat16), (("ping", 0),), REACH).astype(envelope.dtype)
    smoothed = smooth_pings(padded, ping_index * ping_count, ping_total * ping_count, ping_count)
    centroid, energy = window_stats(smoothed, start, length)
    return (centroid, energy)


def beam_kernel(me_ref, x_ref, w_ref, rep_ref, *outs, count, first_band, splits):
    bands = x_ref.shape[2]
    pings, bins, staves = x_ref.shape[1], x_ref.shape[3], x_ref.shape[4]
    rows = pings * bins
    step = pl.program_id(0)
    base = (first_band + step * bands) * bins
    q_rows = lax.broadcasted_iota(jnp.int32, (bins, rep_ref.shape[1]), 0)
    q_cols = lax.broadcasted_iota(jnp.int32, (bins, rep_ref.shape[1]), 1)
    lower = lax.broadcasted_iota(jnp.int32, (2 * bins, LANES), 1) < LANES // PAIR
    swap = jnp.broadcast_to(lax.bitwise_and(me_ref[0], PAIR - 1) == 1, (2 * bins, LANES))
    places = [(i, at) for i, size in enumerate(splits) for at in range(size)]

    def spectra(k):
        def part(which):
            flat = x_ref[which, :, k].astype(jnp.float32).reshape(rows, staves)
            return flat.astype(jnp.bfloat16)

        re, im = part(0), part(1)
        both = jnp.concatenate(
            [jnp.concatenate([re, -im], axis=1), jnp.concatenate([im, re], axis=1)], axis=0
        )
        mine = q_cols == q_rows + (base + k * bins)
        rep = [
            jnp.sum(jnp.where(mine, rep_ref[i : i + 1, :], 0.0), axis=1, keepdims=True)
            for i in range(2)
        ]
        return both, rep

    def compressed(k, both, rep, groups):
        weights = jnp.concatenate(
            [
                jnp.concatenate([w_ref[which, k, :, lanes] for lanes in groups], axis=1)
                for which in range(2)
            ],
            axis=0,
        )
        beam = jnp.dot(both, weights, preferred_element_type=jnp.float32)
        beam = beam.astype(jnp.bfloat16).astype(jnp.float32)
        beam_re = beam[:rows].reshape(pings, bins, beam.shape[1])
        beam_im = beam[rows:].reshape(pings, bins, beam.shape[1])
        return (beam_re * rep[0] + beam_im * rep[1], beam_im * rep[0] - beam_re * rep[1])

    for k in range(0, bands, 2):
        pair = [spectra(k), spectra(k + 1)]
        here = slice(k * bins, (k + 2) * bins)
        there = pl.ds(pl.multiple_of((step * bands + k) * bins, 2 * bins), 2 * bins)
        for near in range(0, count, 2 * PAIR):
            groups = []
            for r in (near, near + PAIR):
                group = lax.shift_right_logical(lax.bitwise_xor(me_ref[0], r), 1)
                groups.append(pl.ds(pl.multiple_of(group * LANES, LANES), LANES))
            done = [compressed(k + i, *pair[i], groups) for i in range(2)]
            for which in range(2):
                joined = jnp.concatenate([done[0][which], done[1][which]], axis=1)
                for part in range(len(groups)):
                    lane = slice(part * LANES, (part + 1) * LANES)
                    r = near + PAIR * part
                    for slot, (i, at) in enumerate(places):
                        one, two = joined[slot, :, lane], joined[pings - 1 - slot, :, lane]
                        first = jnp.where(lower, one, pltpu.roll(two, LANES // PAIR, 1))
                        second = jnp.where(lower, pltpu.roll(one, LANES // PAIR, 1), two)
                        first, second = first.astype(jnp.bfloat16), second.astype(jnp.bfloat16)
                        to = here if r == 0 else there
                        outs[i * count + r][which, at, to, :] = jnp.where(swap, second, first)
                        outs[i * count + r + 1][which, at, there, :] = jnp.where(swap, first, second)


def beamform(me, staves, weights, replica, count, first_band, steps, bands, splits):
    pings, bins = staves.shape[1], staves.shape[3]
    depth, beams = weights.shape[2], weights.shape[3]
    local_q = weights.shape[1] * bins
    skip = first_band // bands
    rows = bands * bins
    shapes = [
        jax.ShapeDtypeStruct((2, size, steps * rows, LANES), jnp.bfloat16)
        for size in splits
        for _ in range(count)
    ]
    flops = 8 * steps * bands * pings * bins * depth * beams
    moved = 4 * steps * bands * depth * beams + 8 * steps * bands * pings * bins * depth
    return pl.pallas_call(
        functools.partial(beam_kernel, count=count, first_band=first_band, splits=splits),
        grid_spec=pltpu.PrefetchScalarGridSpec(
            num_scalar_prefetch=1,
            grid=(steps,),
            in_specs=[
                pl.BlockSpec((2, pings, bands, bins, depth), lambda s, me: (0, 0, skip + s, 0, 0)),
                pl.BlockSpec((2, bands, depth, beams), lambda s, me: (0, skip + s, 0, 0)),
                pl.BlockSpec((2, local_q), lambda s, me: (0, me[0])),
            ],
            out_specs=[
                pl.BlockSpec((2, size, rows, LANES), lambda s, me: (0, 0, s, 0))
                if r == 0
                else pl.BlockSpec(memory_space=pltpu.VMEM)
                for size in splits
                for r in range(count)
            ],
        ),
        out_shape=shapes,
        compiler_params=pltpu.CompilerParams(vmem_limit_bytes=24 << 20),
        cost_estimate=pl.CostEstimate(flops=flops, bytes_accessed=moved, transcendentals=0),
        name="beamform",
    )(me, *(pltpu.with_memory_space_constraint(a, pltpu.HBM) for a in (staves, weights, replica)))


def add(a, b):
    return (a[0] + b[0], a[1] + b[1])


def sub(a, b):
    return (a[0] - b[0], a[1] - b[1])


def turned(z, steps, signs, count):
    cos, sin = 1.0, 0.0
    for bit in range(steps.bit_length()):
        if steps >> bit & 1:
            angle = 2.0 * math.pi * (1 << bit) / count
            quarter = 4 << bit == count
            c, s = 0.0 if quarter else math.cos(angle), signs[bit] * math.sin(angle)
            if quarter:
                cos, sin = (-1.0 * sin * s if not isinstance(sin, float) else 0.0), cos * s
            else:
                cos, sin = c, s
    if isinstance(cos, float) and cos == 0.0:
        return (z[1] * -sin, z[0] * sin)
    return (z[0] * cos - z[1] * sin, z[1] * cos + z[0] * sin)


def small_dft(values, signs):
    count = len(values)
    if count == 1:
        return values
    middle = count // 2
    even = small_dft([add(values[i], values[i + middle]) for i in range(middle)], signs)
    apart = [sub(values[i], values[i + middle]) for i in range(middle)]
    odd = small_dft(
        [apart[0]] + [turned(apart[i], i, signs, count) for i in range(1, middle)], signs
    )
    return [even[i // 2] if i % 2 == 0 else odd[i // 2] for i in range(count)]


def turned_kernel(me_ref, *refs, count, width, together):
    heads, tails = refs[:count], refs[count : 2 * count]
    cos_ref, sin_ref, window_ref, out_ref, spec, power, kept, acc = refs[2 * count :]
    step = pl.program_id(0)
    slots = 2
    head_rows, tail_rows = heads[0].shape[2], tails[0].shape[2]
    depth = head_rows + tail_rows
    signs = [
        (1 - 2 * lax.bitwise_and(lax.shift_right_logical(me_ref[0], b), 1)).astype(jnp.float32)
        for b in range(count.bit_length() - 2)
    ]

    def transform(sources, slot, row, to):
        values = [
            tuple(ref[i, slot, pl.ds(row, BLOCK), :].astype(jnp.float32) for i in range(2))
            for ref in sources
        ]
        for m, z in enumerate(small_dft(values, signs)):
            spec[m, slot, pl.ds(to, BLOCK), :] = z[0].astype(jnp.bfloat16)
            spec[m, slot, pl.ds(depth + to, BLOCK), :] = z[1].astype(jnp.bfloat16)

    @pl.when(step == 0)
    def _():
        acc[...] = jnp.zeros_like(acc)
        for slot in range(slots):

            @pl.loop(0, head_rows // BLOCK)
            def _(i):
                row = pl.multiple_of(i * BLOCK, BLOCK)
                transform(heads, slot, row, row)

            @pl.loop(0, tail_rows // BLOCK)
            def _(i):
                row = pl.multiple_of(i * BLOCK, BLOCK)
                transform(tails, slot, row, pl.multiple_of(head_rows + row, BLOCK))

    for j in range(together):
        m = step * together + j
        cos, sin = cos_ref[j], sin_ref[j]
        table = jnp.concatenate(
            [jnp.concatenate([cos, -sin], axis=1), jnp.concatenate([sin, cos], axis=1)], axis=0
        )
        spectra = jnp.concatenate([spec[m, 0], spec[m, 1]], axis=1)
        wave = jnp.dot(table, spectra, preferred_element_type=jnp.float32)
        power[j] = wave[:depth] * wave[:depth] + wave[depth:] * wave[depth:]

    shift = count.bit_length() - 1
    first_row = lax.broadcasted_iota(jnp.int32, (BLOCK, LANES), 0)
    for j in range(together):
        m = step * together + j
        edges = [
            [
                jnp.broadcast_to(
                    lax.shift_right_arithmetic(window_ref[i, o : o + 1, :] + (count - 1 - m), shift)
                    .astype(jnp.float32)
                    .astype(jnp.bfloat16),
                    (BLOCK, LANES),
                )
                for o in range(width)
            ]
            for i in range(2)
        ]

        def windowed(i, carry):
            row = pl.multiple_of(i * BLOCK, BLOCK)
            one = power[j, pl.ds(row, BLOCK), :LANES]
            two = power[j, pl.ds(row, BLOCK), LANES:]
            both = one + two
            rows = (first_row + row).astype(jnp.float32).astype(jnp.bfloat16)

            def keep(o, value):
                inside = (rows >= edges[0][o]) & (rows < edges[1][o])
                value = jnp.where(inside, value.astype(jnp.bfloat16), jnp.bfloat16(0))
                kept[j, o, pl.ds(row, BLOCK), :] = value

            for o in range(REACH + 1):
                keep(o, one)
                keep(width - 1 - o, two)
                if o < REACH:
                    one, two = one + both, two + both
            return carry

        lax.fori_loop(0, depth // BLOCK, windowed, 0, unroll=2)

    sum_row = lax.broadcasted_iota(jnp.int32, (BLOCK, depth), 0)
    sum_col = lax.broadcasted_iota(jnp.int32, (BLOCK, depth), 1)
    for j in range(together):
        m = step * together + j
        sums = jnp.where(sum_row == 0, 1, jnp.where(sum_row == 1, count * sum_col, 0))
        sums = jnp.where(sum_row == 2, m, sums).astype(jnp.float32).astype(jnp.bfloat16)
        for o in range(0, width, 2):
            pair = jnp.concatenate([kept[j, o], kept[j, o + 1]], axis=1)
            lanes = slice(o * LANES, (o + 2) * LANES)
            acc[:, lanes] += jnp.dot(sums, pair, preferred_element_type=jnp.float32)[:8]

    @pl.when(step == count // together - 1)
    def _():
        out_ref[...] = acc[...]


def window_sums(me, heads, tails, tables, windows, chunk):
    count = len(heads)
    width = 2 * REACH + 2
    together = 2
    head_rows, tail_rows = heads[0].shape[2], tails[0].shape[2]
    depth = head_rows + tail_rows
    flops = 2 * count * (2 * depth) * (2 * depth) * (2 * LANES)
    moved = 4 * tables[0].size + 16 * count * depth * LANES
    sums = pl.pallas_call(
        functools.partial(turned_kernel, count=count, width=width, together=together),
        grid_spec=pltpu.PrefetchScalarGridSpec(
            num_scalar_prefetch=1,
            grid=(count // together,),
            in_specs=[
                pl.BlockSpec((2, 2, head_rows, LANES), lambda s, me: (0, chunk, 0, 0))
                for _ in range(count)
            ]
            + [
                pl.BlockSpec((2, 2, tail_rows, LANES), lambda s, me: (0, 0, 0, 0))
                for _ in range(count)
            ]
            + [pl.BlockSpec((together, depth, depth), lambda s, me: (s, 0, 0)) for _ in range(2)]
            + [pl.BlockSpec((2, width, LANES), lambda s, me: (0, 0, 0))],
            out_specs=pl.BlockSpec((8, width * LANES), lambda s, me: (0, 0)),
            scratch_shapes=[
                pltpu.VMEM((count, 2, 2 * depth, LANES), jnp.bfloat16),
                pltpu.VMEM((together, depth, 2 * LANES), jnp.float32),
                pltpu.VMEM((together, width, depth, LANES), jnp.bfloat16),
                pltpu.VMEM((8, width * LANES), jnp.float32),
            ],
        ),
        out_shape=jax.ShapeDtypeStruct((8, width * LANES), jnp.float32),
        compiler_params=pltpu.CompilerParams(vmem_limit_bytes=14 << 20),
        cost_estimate=pl.CostEstimate(flops=flops, bytes_accessed=moved, transcendentals=0),
        name="window_sums",
    )(me, *heads, *tails, *tables, windows)
    return jnp.stack([sums[0], sums[1] + sums[2]]).reshape(2, width, LANES)


def wave_tables(count, depth, after):
    total = count * depth
    index = jnp.arange(depth, dtype=jnp.int32)
    index, _ = lax.optimization_barrier((index, after))
    angle = ((index[:, None] * index[None, :]) % depth).astype(jnp.float32) * (2.0 * math.pi / depth)
    turn = (jnp.arange(count, dtype=jnp.int32)[:, None] * index[None, :]).astype(jnp.float32)
    turn = turn * (2.0 * math.pi / total)
    small = (jnp.cos(angle), jnp.sin(angle), jnp.cos(turn), jnp.sin(turn))
    cos_a, sin_a, cos_b, sin_b = lax.optimization_barrier(small)
    cos_b, sin_b = cos_b[:, None, :], sin_b[:, None, :]
    cos = (cos_a * cos_b - sin_a * sin_b).astype(jnp.bfloat16)
    sin = (sin_a * cos_b + cos_a * sin_b).astype(jnp.bfloat16)
    return lax.optimization_barrier((cos, sin))


def local_fast(staves, weights, replica, start, length):
    count = lax.axis_size("band")
    blocks = lax.axis_size("ping")
    me = jnp.reshape(lax.axis_index("band"), (1,)).astype(jnp.int32)
    block = lax.axis_index("ping")
    pings, bands, bins = staves.shape[1:4]
    half = pings // PAIR
    chunks = half // 2
    depth = bands * bins
    mine = start.shape[1]

    def send(array, r):
        return lax.ppermute(array, "band", [(i, i ^ r) for i in range(count)])

    def up(array):
        return lax.ppermute(array, "ping", [(i, i + 1) for i in range(blocks - 1)])

    def down(array):
        return lax.ppermute(array, "ping", [(i + 1, i) for i in range(blocks - 1)])

    head_bands = HEAD_STEPS * STEP_BANDS
    heads = beamform(me, staves, weights, replica, count, 0, HEAD_STEPS, STEP_BANDS, (half,))
    got_heads = [heads[0]] + [send(heads[r], r) for r in range(1, count)]

    rest = (bands - head_bands) // (2 * STEP_BANDS)
    me_next, _ = lax.optimization_barrier((me, heads[0]))
    tails = beamform(
        me_next, staves, weights, replica, count, head_bands, rest, 2 * STEP_BANDS, (2,) * chunks
    )
    got_tails = []
    for i in range(chunks):
        own = tails[i * count : (i + 1) * count]
        got_tails.append([own[0]] + [send(own[r], r) for r in range(1, count)])

    own_start, own_length, _ = lax.optimization_barrier((start, length, tails[0]))
    spans = jnp.stack([own_start, own_start + own_length])
    reach = half + REACH
    before = up(spans[:, pings - REACH :])
    after = down(spans[:, :REACH])
    left = jnp.concatenate([before, spans[:, :reach]], axis=1)
    right = jnp.concatenate([spans[:, pings - reach :], after], axis=1)
    windows = jnp.concatenate([left, jnp.flip(right, 1)], axis=2)

    tables = wave_tables(count, depth, tails[0])

    width = 2 * REACH + 2
    reached = half + 2 * REACH
    sums = jnp.zeros((2, reached, LANES), jnp.float32)
    for i in range(chunks):
        reached_windows = windows[:, 2 * i : 2 * i + width]
        if i == chunks - 1:
            reached_windows, edge_left, edge_right = lax.optimization_barrier(
                (reached_windows, edge_left, edge_right)
            )
        part = window_sums(me, got_heads, got_tails[i], tables, reached_windows, i)
        sums = sums + jnp.pad(part, ((0, 0), (2 * i, reached - width - 2 * i), (0, 0)))
        if 2 * (i + 1) == REACH:
            edge_left = down(sums[:, :REACH, :mine])
            edge_right = up(jnp.flip(sums[:, :REACH, mine:], 1))

    def placed(array, before):
        after = pings - before - array.shape[1]
        return jnp.pad(array, ((0, 0), (before, after), (0, 0)))

    whole = placed(sums[:, REACH:, :mine], 0)
    whole = whole + placed(jnp.flip(sums[:, REACH:, mine:], 1), pings - reach)
    whole = whole + placed(edge_left, pings - REACH) + placed(edge_right, 0)

    weight_sum = tap_weights(block * pings, blocks * pings, pings)
    scale = (1.0 / (16.0 * count * depth)) / weight_sum[:, None]
    widths = length.astype(jnp.float32)
    energy_total = whole[0] * scale
    moment = (whole[1] - whole[0] * (start.astype(jnp.float32) - 0.5)) * scale
    return (moment / (widths * (energy_total + 1e-06)), energy_total / widths)


def fits(mesh, staves, weights):
    count, blocks = mesh.shape["band"], mesh.shape["ping"]
    pings, bands = staves.shape[1] // blocks, staves.shape[2] // count
    bins, depth = staves.shape[3:]
    beams = weights.shape[3]
    half = pings // PAIR
    head_bands = HEAD_STEPS * STEP_BANDS
    return (
        count == 8
        and beams * PAIR == LANES * count
        and beams % (2 * LANES) == 0
        and pings % (2 * PAIR) == 0
        and half > REACH
        and bins == 8
        and depth % LANES == 0
        and bands * bins % LANES == 0
        and bands * bins <= 2 * LANES
        and bands > head_bands
        and (bands - head_bands) % (2 * STEP_BANDS) == 0
        and head_bands % (2 * STEP_BANDS) == 0
    )


def solution(mesh):
    in_specs = (
        P(None, "ping", "band", None, None),
        P(None, "band", None, None),
        P(),
        P("ping", "band"),
        P("ping", "band"),
    )
    out_specs = (P("ping", "band"), P("ping", "band"))

    def run(staves, weights, replica, start, length):
        quick = fits(mesh, staves, weights)

        def local(*arrays):
            return (local_fast if quick else local_plain)(*arrays)

        body = jax.shard_map(
            local, mesh=mesh, in_specs=in_specs, out_specs=out_specs, check_vma=False
        )
        return body(staves, weights, replica, start, length)

    return run
```

```python
import functools
import math

import jax
import jax.numpy as jnp
from jax import lax
from jax.experimental import pallas as pl
from jax.experimental.pallas import tpu as pltpu
from jax.sharding import PartitionSpec as P


TAPS = (1.0, 2.0, 3.0, 4.0, 5.0, 4.0, 3.0, 2.0, 1.0)
REACH = len(TAPS) // 2
LANES = 128
PAIR = 2
BLOCK = 16
HEAD_STEPS = 4
STEP_BANDS = 2
SPLITS = (4, 2, 2)


def extended(array, sides, width):
    for axis, dim in sides:
        count, length = (lax.axis_size(axis), array.shape[dim])
        up = [(i, (i + 1) % count) for i in range(count - 1)]
        down = [(j, i) for i, j in up]
        last = lax.slice_in_dim(array, length - width, length, axis=dim)
        initial = lax.slice_in_dim(array, 0, width, axis=dim)
        before = lax.ppermute(last, axis, up)
        after = lax.ppermute(initial, axis, down)
        array = jnp.concatenate([before, array, after], axis=dim)
    return array


def dft_tables(length_total):
    freqs = jnp.arange(length_total, dtype=jnp.int32)
    phases = freqs[:, None] * freqs[None, :] % length_total
    angles = phases.astype(jnp.float32) * (2.0 * math.pi / length_total)
    return (jnp.cos(angles).astype(jnp.bfloat16), jnp.sin(angles).astype(jnp.bfloat16))


def envelope_rows(spec_re, spec_im, replica, cos_table, sin_table):
    comp_re = (spec_re * replica[0] + spec_im * replica[1]).astype(jnp.bfloat16)
    comp_im = (spec_im * replica[0] - spec_re * replica[1]).astype(jnp.bfloat16)
    wave_re = jnp.dot(comp_re, cos_table, preferred_element_type=jnp.float32) - jnp.dot(
        comp_im, sin_table, preferred_element_type=jnp.float32
    )
    wave_im = jnp.dot(comp_re, sin_table, preferred_element_type=jnp.float32) + jnp.dot(
        comp_im, cos_table, preferred_element_type=jnp.float32
    )
    return (wave_re * wave_re + wave_im * wave_im) * (1.0 / (16.0 * cos_table.shape[0]))


def tap_weights(first_ping, total_pings, ping_count):
    positions = first_ping + jnp.arange(ping_count + 2 * REACH, dtype=jnp.int32) - REACH
    inside = ((positions >= 0) & (positions < total_pings)).astype(jnp.float32)
    weight_sum = jnp.zeros((ping_count,), jnp.float32)
    for offset, tap in enumerate(TAPS):
        weight_sum = weight_sum + tap * inside[offset : offset + ping_count]
    return weight_sum


def smooth_pings(padded, first_ping, total_pings, ping_count):
    summed = jnp.zeros((ping_count,) + padded.shape[1:], jnp.float32)
    for offset, tap in enumerate(TAPS):
        summed = summed + tap * padded[offset : offset + ping_count]
    return summed / tap_weights(first_ping, total_pings, ping_count)[:, None, None]


def window_stats(smoothed, start, length):
    samples = jnp.arange(smoothed.shape[-1], dtype=jnp.int32)
    window_start = start[..., None]
    finish = (start + length)[..., None]
    inside = (samples >= window_start) & (samples < finish)
    offsets = samples.astype(jnp.float32) - start.astype(jnp.float32)[..., None] + 0.5
    energy_total = jnp.sum(jnp.where(inside, smoothed, 0.0), axis=-1)
    moment = jnp.sum(jnp.where(inside, smoothed * offsets, 0.0), axis=-1)
    widths = length.astype(jnp.float32)
    return (moment / (widths * (energy_total + 1e-06)), energy_total / widths)


def local_plain(staves, weights, replica, start, length):
    ping_index = lax.axis_index("ping")
    ping_total = lax.axis_size("ping")
    beam_re = jnp.einsum(
        "pkfs,ksb->kpfb", staves[0], weights[0], preferred_element_type=jnp.float32
    ) - jnp.einsum("pkfs,ksb->kpfb", staves[1], weights[1], preferred_element_type=jnp.float32)
    beam_im = jnp.einsum(
        "pkfs,ksb->kpfb", staves[0], weights[1], preferred_element_type=jnp.float32
    ) + jnp.einsum("pkfs,ksb->kpfb", staves[1], weights[0], preferred_element_type=jnp.float32)
    beams = jnp.stack([beam_re, beam_im]).astype(jnp.bfloat16)
    cos_table, sin_table = dft_tables(replica.shape[1])
    turned = lax.all_to_all(beams, "band", split_axis=4, concat_axis=1, tiled=True)
    pings_here = turned.shape[2]
    beams_here = turned.shape[4]
    flat_rows = jnp.transpose(turned, (0, 2, 4, 1, 3)).reshape(2, pings_here * beams_here, -1)
    energy_rows = envelope_rows(
        flat_rows[0].astype(jnp.float32),
        flat_rows[1].astype(jnp.float32),
        replica,
        cos_table,
        sin_table,
    )
    envelope = energy_rows.reshape(pings_here, beams_here, -1)
    ping_count = envelope.shape[0]
    padded = extended(envelope.astype(jnp.bfloat16), (("ping", 0),), REACH).astype(envelope.dtype)
    smoothed = smooth_pings(padded, ping_index * ping_count, ping_total * ping_count, ping_count)
    centroid, energy = window_stats(smoothed, start, length)
    return (centroid, energy)


def beam_kernel(me_ref, x_ref, w_ref, rep_ref, *outs, count, first_band, splits):
    bands = x_ref.shape[2]
    pings, bins, staves = x_ref.shape[1], x_ref.shape[3], x_ref.shape[4]
    rows = pings * bins
    step = pl.program_id(0)
    base = (first_band + step * bands) * bins
    q_rows = lax.broadcasted_iota(jnp.int32, (bins, rep_ref.shape[1]), 0)
    q_cols = lax.broadcasted_iota(jnp.int32, (bins, rep_ref.shape[1]), 1)
    lower = lax.broadcasted_iota(jnp.int32, (2 * bins, LANES), 1) < LANES // PAIR
    swap = jnp.broadcast_to(lax.bitwise_and(me_ref[0], PAIR - 1) == 1, (2 * bins, LANES))
    places = [(i, at) for i, size in enumerate(splits) for at in range(size)]

    def spectra(k):
        def part(which):
            flat = x_ref[which, :, k].astype(jnp.float32).reshape(rows, staves)
            return flat.astype(jnp.bfloat16)

        re, im = part(0), part(1)
        both = jnp.concatenate(
            [jnp.concatenate([re, -im], axis=1), jnp.concatenate([im, re], axis=1)], axis=0
        )
        mine = q_cols == q_rows + (base + k * bins)
        rep = [
            jnp.sum(jnp.where(mine, rep_ref[i : i + 1, :], 0.0), axis=1, keepdims=True)
            for i in range(2)
        ]
        return both, rep

    def compressed(k, both, rep, groups):
        weights = jnp.concatenate(
            [
                jnp.concatenate([w_ref[which, k, :, lanes] for lanes in groups], axis=1)
                for which in range(2)
            ],
            axis=0,
        )
        beam = jnp.dot(both, weights, preferred_element_type=jnp.float32)
        beam = beam.astype(jnp.bfloat16).astype(jnp.float32)
        beam_re = beam[:rows].reshape(pings, bins, beam.shape[1])
        beam_im = beam[rows:].reshape(pings, bins, beam.shape[1])
        return (beam_re * rep[0] + beam_im * rep[1], beam_im * rep[0] - beam_re * rep[1])

    for k in range(0, bands, 2):
        pair = [spectra(k), spectra(k + 1)]
        here = slice(k * bins, (k + 2) * bins)
        for near in range(0, count, 2 * PAIR):
            groups = []
            for r in (near, near + PAIR):
                group = lax.shift_right_logical(lax.bitwise_xor(me_ref[0], r), 1)
                groups.append(pl.ds(pl.multiple_of(group * LANES, LANES), LANES))
            done = [compressed(k + i, *pair[i], groups) for i in range(2)]
            for which in range(2):
                joined = jnp.concatenate([done[0][which], done[1][which]], axis=1)
                for part in range(len(groups)):
                    lane = slice(part * LANES, (part + 1) * LANES)
                    r = near + PAIR * part
                    for slot, (i, at) in enumerate(places):
                        one, two = joined[slot, :, lane], joined[pings - 1 - slot, :, lane]
                        first = jnp.where(lower, one, pltpu.roll(two, LANES // PAIR, 1))
                        second = jnp.where(lower, pltpu.roll(one, LANES // PAIR, 1), two)
                        first, second = first.astype(jnp.bfloat16), second.astype(jnp.bfloat16)
                        outs[i * count + r][which, at, here] = jnp.where(swap, second, first)
                        outs[i * count + r + 1][which, at, here] = jnp.where(swap, first, second)


def in_place(array):
    return pltpu.with_memory_space_constraint(array, pltpu.HBM)


def beamform(me, staves, weights, replica, count, first_band, steps, bands, splits):
    pings, bins = staves.shape[1], staves.shape[3]
    depth, beams = weights.shape[2], weights.shape[3]
    local_q = weights.shape[1] * bins
    skip = first_band // bands
    rows = bands * bins
    shapes = [
        pltpu.HBM((2, size, steps * rows, LANES), jnp.bfloat16)
        for size in splits
        for _ in range(count)
    ]
    flops = 8 * steps * bands * pings * bins * depth * beams
    moved = 4 * steps * bands * depth * beams + 8 * steps * bands * pings * bins * depth
    return pl.pallas_call(
        functools.partial(beam_kernel, count=count, first_band=first_band, splits=splits),
        grid_spec=pltpu.PrefetchScalarGridSpec(
            num_scalar_prefetch=1,
            grid=(steps,),
            in_specs=[
                pl.BlockSpec((2, pings, bands, bins, depth), lambda s, me: (0, 0, skip + s, 0, 0)),
                pl.BlockSpec((2, bands, depth, beams), lambda s, me: (0, skip + s, 0, 0)),
                pl.BlockSpec((2, local_q), lambda s, me: (0, me[0])),
            ],
            out_specs=[
                pl.BlockSpec((2, size, rows, LANES), lambda s, me: (0, 0, s, 0))
                for size in splits
                for _ in range(count)
            ],
        ),
        out_shape=shapes,
        compiler_params=pltpu.CompilerParams(vmem_limit_bytes=24 << 20),
        cost_estimate=pl.CostEstimate(flops=flops, bytes_accessed=moved, transcendentals=0),
        name="beamform",
    )(me, in_place(staves), in_place(weights), in_place(replica))


def add(a, b):
    return (a[0] + b[0], a[1] + b[1])


def sub(a, b):
    return (a[0] - b[0], a[1] - b[1])


def turned(z, steps, signs, count):
    cos, sin = 1.0, 0.0
    for bit in range(steps.bit_length()):
        if steps >> bit & 1:
            angle = 2.0 * math.pi * (1 << bit) / count
            quarter = 4 << bit == count
            c, s = 0.0 if quarter else math.cos(angle), signs[bit] * math.sin(angle)
            if quarter:
                cos, sin = (-1.0 * sin * s if not isinstance(sin, float) else 0.0), cos * s
            else:
                cos, sin = c, s
    if isinstance(cos, float) and cos == 0.0:
        return (z[1] * -sin, z[0] * sin)
    return (z[0] * cos - z[1] * sin, z[1] * cos + z[0] * sin)


def small_dft(values, signs):
    count = len(values)
    if count == 1:
        return values
    middle = count // 2
    even = small_dft([add(values[i], values[i + middle]) for i in range(middle)], signs)
    apart = [sub(values[i], values[i + middle]) for i in range(middle)]
    odd = small_dft(
        [apart[0]] + [turned(apart[i], i, signs, count) for i in range(1, middle)], signs
    )
    return [even[i // 2] if i % 2 == 0 else odd[i // 2] for i in range(count)]


def five_wide(values):
    known = {}

    def run(first, size):
        if size == 1:
            return values[first]
        if (first, size) not in known:
            part = 1 << (size - 1).bit_length() - 1
            known[first, size] = run(first, part) + run(first + part, size - part)
        return known[first, size]

    count = len(values)
    ends = [(max(0, i - REACH), min(count, i + 1)) for i in range(count + REACH)]
    return [run(first, last - first) for first, last in ends]


def turned_kernel(me_ref, *refs, count, slots, together):
    heads, tails = refs[:count], refs[count : 2 * count]
    cos_ref, sin_ref, window_ref, out_ref, spec, power, kept, acc = refs[2 * count :]
    step = pl.program_id(0)
    width = 2 * REACH + slots
    head_rows, tail_rows = heads[0].shape[2], tails[0].shape[2]
    depth = head_rows + tail_rows
    signs = [
        (1 - 2 * lax.bitwise_and(lax.shift_right_logical(me_ref[0], b), 1)).astype(jnp.float32)
        for b in range(count.bit_length() - 2)
    ]

    def transform(sources, slot, row, to):
        values = [
            tuple(ref[i, slot, pl.ds(row, BLOCK), :].astype(jnp.float32) for i in range(2))
            for ref in sources
        ]
        for m, z in enumerate(small_dft(values, signs)):
            spec[m, slot, pl.ds(to, BLOCK), :] = z[0].astype(jnp.bfloat16)
            spec[m, slot, pl.ds(depth + to, BLOCK), :] = z[1].astype(jnp.bfloat16)

    @pl.when(step == 0)
    def _():
        acc[...] = jnp.zeros_like(acc)
        for slot in range(slots):

            @pl.loop(0, head_rows // BLOCK)
            def _(i):
                row = pl.multiple_of(i * BLOCK, BLOCK)
                transform(heads, slot, row, row)

            @pl.loop(0, tail_rows // BLOCK)
            def _(i):
                row = pl.multiple_of(i * BLOCK, BLOCK)
                transform(tails, slot, row, pl.multiple_of(head_rows + row, BLOCK))

    for j in range(together):
        m = step * together + j
        cos, sin = cos_ref[j], sin_ref[j]
        table = jnp.concatenate(
            [jnp.concatenate([cos, -sin], axis=1), jnp.concatenate([sin, cos], axis=1)], axis=0
        )
        for slot in range(0, slots, 2):
            spectra = jnp.concatenate([spec[m, slot], spec[m, slot + 1]], axis=1)
            wave = jnp.dot(table, spectra, preferred_element_type=jnp.float32)
            lanes = slice(slot * LANES, (slot + 2) * LANES)
            power[j, :, lanes] = wave[:depth] * wave[:depth] + wave[depth:] * wave[depth:]

    first_row = lax.broadcasted_iota(jnp.int32, (BLOCK, LANES), 0)
    for j in range(together):

        def windowed(i, carry):
            row = pl.multiple_of(i * BLOCK, BLOCK)
            rows = (first_row + row).astype(jnp.float32).astype(jnp.bfloat16)
            values = [
                power[j, pl.ds(row, BLOCK), slot * LANES : (slot + 1) * LANES]
                for slot in range(slots)
            ]
            for o, value in enumerate(five_wide(five_wide(values))):
                inside = (rows >= window_ref[j, 0, o]) & (rows < window_ref[j, 1, o])
                value = jnp.where(inside, value.astype(jnp.bfloat16), jnp.bfloat16(0))
                kept[j, o, pl.ds(row, BLOCK), :] = value
            return carry

        lax.fori_loop(0, depth // BLOCK, windowed, 0, unroll=2)

    sum_row = lax.broadcasted_iota(jnp.int32, (BLOCK, depth), 0)
    sum_col = lax.broadcasted_iota(jnp.int32, (BLOCK, depth), 1)
    for j in range(together):
        m = step * together + j
        sums = jnp.where(sum_row == 0, 1, jnp.where(sum_row == 1, count * sum_col, 0))
        sums = jnp.where(sum_row == 2, m, sums).astype(jnp.float32).astype(jnp.bfloat16)
        for o in range(0, width, 2):
            pair = jnp.concatenate([kept[j, o], kept[j, o + 1]], axis=1)
            lanes = slice(o * LANES, (o + 2) * LANES)
            acc[:, lanes] += jnp.dot(sums, pair, preferred_element_type=jnp.float32)[:8]

    @pl.when(step == count // together - 1)
    def _():
        out_ref[...] = acc[...]


def window_sums(me, heads, tails, tables, windows, first_slot):
    count = len(heads)
    slots = tails[0].shape[1]
    chunk = first_slot // slots
    width = 2 * REACH + slots
    together = 2
    head_rows, tail_rows = heads[0].shape[2], tails[0].shape[2]
    depth = head_rows + tail_rows
    flops = 2 * count * (2 * depth) * (2 * depth) * (slots * LANES)
    moved = 4 * tables[0].size + 16 * count * depth * LANES
    sums = pl.pallas_call(
        functools.partial(turned_kernel, count=count, slots=slots, together=together),
        grid_spec=pltpu.PrefetchScalarGridSpec(
            num_scalar_prefetch=1,
            grid=(count // together,),
            in_specs=[
                pl.BlockSpec((2, slots, head_rows, LANES), lambda s, me: (0, chunk, 0, 0))
                for _ in range(count)
            ]
            + [
                pl.BlockSpec((2, slots, tail_rows, LANES), lambda s, me: (0, 0, 0, 0))
                for _ in range(count)
            ]
            + [pl.BlockSpec((together, depth, depth), lambda s, me: (s, 0, 0)) for _ in range(2)]
            + [pl.BlockSpec((together, 2, width, BLOCK, LANES), lambda s, me: (s, 0, 0, 0, 0))],
            out_specs=pl.BlockSpec((8, width * LANES), lambda s, me: (0, 0)),
            scratch_shapes=[
                pltpu.VMEM((count, slots, 2 * depth, LANES), jnp.bfloat16),
                pltpu.VMEM((together, depth, slots * LANES), jnp.float32),
                pltpu.VMEM((together, width, depth, LANES), jnp.bfloat16),
                pltpu.VMEM((8, width * LANES), jnp.float32),
            ],
        ),
        out_shape=jax.ShapeDtypeStruct((8, width * LANES), jnp.float32),
        compiler_params=pltpu.CompilerParams(vmem_limit_bytes=(6 + 4 * slots) << 20),
        cost_estimate=pl.CostEstimate(flops=flops, bytes_accessed=moved, transcendentals=0),
        name="window_sums",
    )(me, in_place(heads[0]), *heads[1:], in_place(tails[0]), *tails[1:], *tables, windows)
    return jnp.stack([sums[0], sums[1] + sums[2]]).reshape(2, width, LANES)


def wave_tables(count, depth, after):
    total = count * depth
    index = jnp.arange(depth, dtype=jnp.int32)
    index, _ = lax.optimization_barrier((index, after))
    angle = ((index[:, None] * index[None, :]) % depth).astype(jnp.float32) * (2.0 * math.pi / depth)
    turn = (jnp.arange(count, dtype=jnp.int32)[:, None] * index[None, :]).astype(jnp.float32)
    turn = turn * (2.0 * math.pi / total)
    small = (jnp.cos(angle), jnp.sin(angle), jnp.cos(turn), jnp.sin(turn))
    cos_a, sin_a, cos_b, sin_b = lax.optimization_barrier(small)
    cos_b, sin_b = cos_b[:, None, :], sin_b[:, None, :]
    cos = (cos_a * cos_b - sin_a * sin_b).astype(jnp.bfloat16)
    sin = (sin_a * cos_b + cos_a * sin_b).astype(jnp.bfloat16)
    return lax.optimization_barrier((cos, sin))


def local_fast(staves, weights, replica, start, length):
    count = lax.axis_size("band")
    blocks = lax.axis_size("ping")
    me = jnp.reshape(lax.axis_index("band"), (1,)).astype(jnp.int32)
    block = lax.axis_index("ping")
    pings, bands, bins = staves.shape[1:4]
    half = pings // PAIR
    sizes = SPLITS
    depth = bands * bins
    mine = start.shape[1]

    def send(array, r):
        return lax.ppermute(array, "band", [(i, i ^ r) for i in range(count)])

    def up(array):
        return lax.ppermute(array, "ping", [(i, i + 1) for i in range(blocks - 1)])

    def down(array):
        return lax.ppermute(array, "ping", [(i + 1, i) for i in range(blocks - 1)])

    head_bands = HEAD_STEPS * STEP_BANDS
    heads = beamform(me, staves, weights, replica, count, 0, HEAD_STEPS, STEP_BANDS, (half,))
    got_heads = [heads[0]] + [send(heads[r], r) for r in range(1, count)]

    rest = (bands - head_bands) // (2 * STEP_BANDS)
    me_next, _ = lax.optimization_barrier((me, heads[0]))
    tails = beamform(
        me_next, staves, weights, replica, count, head_bands, rest, 2 * STEP_BANDS, sizes
    )
    got_tails = []
    for i in range(len(sizes)):
        own = tails[i * count : (i + 1) * count]
        got_tails.append([own[0]] + [send(own[r], r) for r in range(1, count)])

    own_start, own_length, _ = lax.optimization_barrier((start, length, tails[0]))
    spans = jnp.stack([own_start, own_start + own_length])
    reach = half + REACH
    before = up(spans[:, pings - REACH :])
    after = down(spans[:, :REACH])
    left = jnp.concatenate([before, spans[:, :reach]], axis=1)
    right = jnp.concatenate([spans[:, pings - reach :], after], axis=1)
    windows = jnp.concatenate([left, jnp.flip(right, 1)], axis=2)
    phase = jnp.arange(count, dtype=jnp.int32)[:, None, None, None]
    windows = lax.div(windows[None] + (count - 1 - phase), count).astype(jnp.bfloat16)
    windows = jnp.broadcast_to(
        windows[:, :, :, None, :], windows.shape[:3] + (BLOCK, windows.shape[3])
    )

    tables = wave_tables(count, depth, tails[0])

    reached = half + 2 * REACH
    sums = jnp.zeros((2, reached, LANES), jnp.float32)
    slot = 0
    for i, size in enumerate(sizes):
        width = 2 * REACH + size
        near = windows[:, :, slot : slot + width]
        part = window_sums(me, got_heads, got_tails[i], tables, near, slot)
        sums = sums + jnp.pad(part, ((0, 0), (slot, reached - width - slot), (0, 0)))
        if slot < REACH <= slot + size:
            edge_left = down(sums[:, :REACH, :mine])
            edge_right = up(jnp.flip(sums[:, :REACH, mine:], 1))
        slot += size

    def placed(array, before):
        after = pings - before - array.shape[1]
        return jnp.pad(array, ((0, 0), (before, after), (0, 0)))

    whole = placed(sums[:, REACH:, :mine], 0)
    whole = whole + placed(jnp.flip(sums[:, REACH:, mine:], 1), pings - reach)
    whole = whole + placed(edge_left, pings - REACH) + placed(edge_right, 0)

    weight_sum = tap_weights(block * pings, blocks * pings, pings)
    scale = (1.0 / (16.0 * count * depth)) / weight_sum[:, None]
    widths = length.astype(jnp.float32)
    energy_total = whole[0] * scale
    moment = (whole[1] - whole[0] * (start.astype(jnp.float32) - 0.5)) * scale
    return (moment / (widths * (energy_total + 1e-06)), energy_total / widths)


def fits(mesh, staves, weights):
    count, blocks = mesh.shape["band"], mesh.shape["ping"]
    pings, bands = staves.shape[1] // blocks, staves.shape[2] // count
    bins, depth = staves.shape[3:]
    beams = weights.shape[3]
    half = pings // PAIR
    head_bands = HEAD_STEPS * STEP_BANDS
    return (
        count == 8
        and beams * PAIR == LANES * count
        and beams % (2 * LANES) == 0
        and pings % (2 * PAIR) == 0
        and half == sum(SPLITS)
        and bins == 8
        and depth % LANES == 0
        and bands * bins % LANES == 0
        and bands * bins <= 2 * LANES
        and bands > head_bands
        and (bands - head_bands) % (2 * STEP_BANDS) == 0
        and head_bands % (2 * STEP_BANDS) == 0
    )


def solution(mesh):
    in_specs = (
        P(None, "ping", "band", None, None),
        P(None, "band", None, None),
        P(),
        P("ping", "band"),
        P("ping", "band"),
    )
    out_specs = (P("ping", "band"), P("ping", "band"))

    def run(staves, weights, replica, start, length):
        quick = fits(mesh, staves, weights)

        def local(*arrays):
            return (local_fast if quick else local_plain)(*arrays)

        body = jax.shard_map(
            local, mesh=mesh, in_specs=in_specs, out_specs=out_specs, check_vma=False
        )
        return body(staves, weights, replica, start, length)

    return run
```

```python
import functools
import math

import jax
import jax.numpy as jnp
from jax import lax
from jax.experimental import pallas as pl
from jax.experimental.pallas import tpu as pltpu
from jax.sharding import PartitionSpec as P


TAPS = (1.0, 2.0, 3.0, 4.0, 5.0, 4.0, 3.0, 2.0, 1.0)
REACH = len(TAPS) // 2
LANES = 128
PAIR = 2
BLOCK = 16
HEAD_STEPS = 4
STEP_BANDS = 2
SPLITS = (5, 2, 1)


def extended(array, sides, width):
    for axis, dim in sides:
        count, length = (lax.axis_size(axis), array.shape[dim])
        up = [(i, (i + 1) % count) for i in range(count - 1)]
        down = [(j, i) for i, j in up]
        last = lax.slice_in_dim(array, length - width, length, axis=dim)
        initial = lax.slice_in_dim(array, 0, width, axis=dim)
        before = lax.ppermute(last, axis, up)
        after = lax.ppermute(initial, axis, down)
        array = jnp.concatenate([before, array, after], axis=dim)
    return array


def dft_tables(length_total):
    freqs = jnp.arange(length_total, dtype=jnp.int32)
    phases = freqs[:, None] * freqs[None, :] % length_total
    angles = phases.astype(jnp.float32) * (2.0 * math.pi / length_total)
    return (jnp.cos(angles).astype(jnp.bfloat16), jnp.sin(angles).astype(jnp.bfloat16))


def envelope_rows(spec_re, spec_im, replica, cos_table, sin_table):
    comp_re = (spec_re * replica[0] + spec_im * replica[1]).astype(jnp.bfloat16)
    comp_im = (spec_im * replica[0] - spec_re * replica[1]).astype(jnp.bfloat16)
    wave_re = jnp.dot(comp_re, cos_table, preferred_element_type=jnp.float32) - jnp.dot(
        comp_im, sin_table, preferred_element_type=jnp.float32
    )
    wave_im = jnp.dot(comp_re, sin_table, preferred_element_type=jnp.float32) + jnp.dot(
        comp_im, cos_table, preferred_element_type=jnp.float32
    )
    return (wave_re * wave_re + wave_im * wave_im) * (1.0 / (16.0 * cos_table.shape[0]))


def tap_weights(first_ping, total_pings, ping_count):
    positions = first_ping + jnp.arange(ping_count + 2 * REACH, dtype=jnp.int32) - REACH
    inside = ((positions >= 0) & (positions < total_pings)).astype(jnp.float32)
    weight_sum = jnp.zeros((ping_count,), jnp.float32)
    for offset, tap in enumerate(TAPS):
        weight_sum = weight_sum + tap * inside[offset : offset + ping_count]
    return weight_sum


def smooth_pings(padded, first_ping, total_pings, ping_count):
    summed = jnp.zeros((ping_count,) + padded.shape[1:], jnp.float32)
    for offset, tap in enumerate(TAPS):
        summed = summed + tap * padded[offset : offset + ping_count]
    return summed / tap_weights(first_ping, total_pings, ping_count)[:, None, None]


def window_stats(smoothed, start, length):
    samples = jnp.arange(smoothed.shape[-1], dtype=jnp.int32)
    window_start = start[..., None]
    finish = (start + length)[..., None]
    inside = (samples >= window_start) & (samples < finish)
    offsets = samples.astype(jnp.float32) - start.astype(jnp.float32)[..., None] + 0.5
    energy_total = jnp.sum(jnp.where(inside, smoothed, 0.0), axis=-1)
    moment = jnp.sum(jnp.where(inside, smoothed * offsets, 0.0), axis=-1)
    widths = length.astype(jnp.float32)
    return (moment / (widths * (energy_total + 1e-06)), energy_total / widths)


def local_plain(staves, weights, replica, start, length):
    ping_index = lax.axis_index("ping")
    ping_total = lax.axis_size("ping")
    beam_re = jnp.einsum(
        "pkfs,ksb->kpfb", staves[0], weights[0], preferred_element_type=jnp.float32
    ) - jnp.einsum("pkfs,ksb->kpfb", staves[1], weights[1], preferred_element_type=jnp.float32)
    beam_im = jnp.einsum(
        "pkfs,ksb->kpfb", staves[0], weights[1], preferred_element_type=jnp.float32
    ) + jnp.einsum("pkfs,ksb->kpfb", staves[1], weights[0], preferred_element_type=jnp.float32)
    beams = jnp.stack([beam_re, beam_im]).astype(jnp.bfloat16)
    cos_table, sin_table = dft_tables(replica.shape[1])
    turned = lax.all_to_all(beams, "band", split_axis=4, concat_axis=1, tiled=True)
    pings_here = turned.shape[2]
    beams_here = turned.shape[4]
    flat_rows = jnp.transpose(turned, (0, 2, 4, 1, 3)).reshape(2, pings_here * beams_here, -1)
    energy_rows = envelope_rows(
        flat_rows[0].astype(jnp.float32),
        flat_rows[1].astype(jnp.float32),
        replica,
        cos_table,
        sin_table,
    )
    envelope = energy_rows.reshape(pings_here, beams_here, -1)
    ping_count = envelope.shape[0]
    padded = extended(envelope.astype(jnp.bfloat16), (("ping", 0),), REACH).astype(envelope.dtype)
    smoothed = smooth_pings(padded, ping_index * ping_count, ping_total * ping_count, ping_count)
    centroid, energy = window_stats(smoothed, start, length)
    return (centroid, energy)


def beam_kernel(me_ref, x_ref, w_ref, rep_ref, *outs, count, first_band, splits):
    bands = x_ref.shape[2]
    pings, bins, staves = x_ref.shape[1], x_ref.shape[3], x_ref.shape[4]
    rows = pings * bins
    step = pl.program_id(0)
    base = (first_band + step * bands) * bins
    q_rows = lax.broadcasted_iota(jnp.int32, (bins, rep_ref.shape[1]), 0)
    q_cols = lax.broadcasted_iota(jnp.int32, (bins, rep_ref.shape[1]), 1)
    lower = lax.broadcasted_iota(jnp.int32, (2 * bins, LANES), 1) < LANES // PAIR
    swap = jnp.broadcast_to(lax.bitwise_and(me_ref[0], PAIR - 1) == 1, (2 * bins, LANES))
    places = [(i, at) for i, size in enumerate(splits) for at in range(size)]

    def spectra(k):
        def part(which):
            flat = x_ref[which, :, k].astype(jnp.float32).reshape(rows, staves)
            return flat.astype(jnp.bfloat16)

        re, im = part(0), part(1)
        both = jnp.concatenate(
            [jnp.concatenate([re, -im], axis=1), jnp.concatenate([im, re], axis=1)], axis=0
        )
        mine = q_cols == q_rows + (base + k * bins)
        rep = [
            jnp.sum(jnp.where(mine, rep_ref[i : i + 1, :], 0.0), axis=1, keepdims=True)
            for i in range(2)
        ]
        return both, rep

    def compressed(k, both, rep, groups):
        weights = jnp.concatenate(
            [
                jnp.concatenate([w_ref[which, k, :, lanes] for lanes in groups], axis=1)
                for which in range(2)
            ],
            axis=0,
        )
        beam = jnp.dot(both, weights, preferred_element_type=jnp.float32)
        beam = beam.astype(jnp.bfloat16).astype(jnp.float32)
        beam_re = beam[:rows].reshape(pings, bins, beam.shape[1])
        beam_im = beam[rows:].reshape(pings, bins, beam.shape[1])
        return (beam_re * rep[0] + beam_im * rep[1], beam_im * rep[0] - beam_re * rep[1])

    for k in range(0, bands, 2):
        pair = [spectra(k), spectra(k + 1)]
        here = slice(k * bins, (k + 2) * bins)
        for near in range(0, count, 2 * PAIR):
            groups = []
            for r in (near, near + PAIR):
                group = lax.shift_right_logical(lax.bitwise_xor(me_ref[0], r), 1)
                groups.append(pl.ds(pl.multiple_of(group * LANES, LANES), LANES))
            done = [compressed(k + i, *pair[i], groups) for i in range(2)]
            for which in range(2):
                joined = jnp.concatenate([done[0][which], done[1][which]], axis=1)
                for part in range(len(groups)):
                    lane = slice(part * LANES, (part + 1) * LANES)
                    r = near + PAIR * part
                    for slot, (i, at) in enumerate(places):
                        one, two = joined[slot, :, lane], joined[pings - 1 - slot, :, lane]
                        first = jnp.where(lower, one, pltpu.roll(two, LANES // PAIR, 1))
                        second = jnp.where(lower, pltpu.roll(one, LANES // PAIR, 1), two)
                        first, second = first.astype(jnp.bfloat16), second.astype(jnp.bfloat16)
                        outs[i * count + r][which, at, here] = jnp.where(swap, second, first)
                        outs[i * count + r + 1][which, at, here] = jnp.where(swap, first, second)


def in_place(array):
    return pltpu.with_memory_space_constraint(array, pltpu.HBM)


def beamform(me, staves, weights, replica, count, first_band, steps, bands, splits):
    pings, bins = staves.shape[1], staves.shape[3]
    depth, beams = weights.shape[2], weights.shape[3]
    local_q = weights.shape[1] * bins
    skip = first_band // bands
    rows = bands * bins
    shapes = [
        pltpu.HBM((2, size, steps * rows, LANES), jnp.bfloat16)
        for size in splits
        for _ in range(count)
    ]
    flops = 8 * steps * bands * pings * bins * depth * beams
    moved = 4 * steps * bands * depth * beams + 8 * steps * bands * pings * bins * depth
    return pl.pallas_call(
        functools.partial(beam_kernel, count=count, first_band=first_band, splits=splits),
        grid_spec=pltpu.PrefetchScalarGridSpec(
            num_scalar_prefetch=1,
            grid=(steps,),
            in_specs=[
                pl.BlockSpec((2, pings, bands, bins, depth), lambda s, me: (0, 0, skip + s, 0, 0)),
                pl.BlockSpec((2, bands, depth, beams), lambda s, me: (0, skip + s, 0, 0)),
                pl.BlockSpec((2, local_q), lambda s, me: (0, me[0])),
            ],
            out_specs=[
                pl.BlockSpec((2, size, rows, LANES), lambda s, me: (0, 0, s, 0))
                for size in splits
                for _ in range(count)
            ],
        ),
        out_shape=shapes,
        compiler_params=pltpu.CompilerParams(vmem_limit_bytes=24 << 20),
        cost_estimate=pl.CostEstimate(flops=flops, bytes_accessed=moved, transcendentals=0),
        name="beamform",
    )(me, in_place(staves), in_place(weights), in_place(replica))


def add(a, b):
    return (a[0] + b[0], a[1] + b[1])


def sub(a, b):
    return (a[0] - b[0], a[1] - b[1])


def turned(z, steps, signs, count):
    cos, sin = 1.0, 0.0
    for bit in range(steps.bit_length()):
        if steps >> bit & 1:
            angle = 2.0 * math.pi * (1 << bit) / count
            quarter = 4 << bit == count
            c, s = 0.0 if quarter else math.cos(angle), signs[bit] * math.sin(angle)
            if quarter:
                cos, sin = (-1.0 * sin * s if not isinstance(sin, float) else 0.0), cos * s
            else:
                cos, sin = c, s
    if isinstance(cos, float) and cos == 0.0:
        return (z[1] * -sin, z[0] * sin)
    return (z[0] * cos - z[1] * sin, z[1] * cos + z[0] * sin)


def small_dft(values, signs):
    count = len(values)
    if count == 1:
        return values
    middle = count // 2
    even = small_dft([add(values[i], values[i + middle]) for i in range(middle)], signs)
    apart = [sub(values[i], values[i + middle]) for i in range(middle)]
    odd = small_dft(
        [apart[0]] + [turned(apart[i], i, signs, count) for i in range(1, middle)], signs
    )
    return [even[i // 2] if i % 2 == 0 else odd[i // 2] for i in range(count)]


def five_wide(values):
    known = {}

    def run(first, size):
        if size == 1:
            return values[first]
        if (first, size) not in known:
            part = 1 << (size - 1).bit_length() - 1
            known[first, size] = run(first, part) + run(first + part, size - part)
        return known[first, size]

    count = len(values)
    ends = [(max(0, i - REACH), min(count, i + 1)) for i in range(count + REACH)]
    return [run(first, last - first) for first, last in ends]


def turned_kernel(me_ref, *refs, count, slots, together):
    heads, tails = refs[:count], refs[count : 2 * count]
    cos_ref, sin_ref, window_ref, out_ref, spec, power, kept, acc = refs[2 * count :]
    step = pl.program_id(0)
    width = 2 * REACH + slots
    head_rows, tail_rows = heads[0].shape[2], tails[0].shape[2]
    depth = head_rows + tail_rows
    signs = [
        (1 - 2 * lax.bitwise_and(lax.shift_right_logical(me_ref[0], b), 1)).astype(jnp.float32)
        for b in range(count.bit_length() - 2)
    ]

    def transform(sources, slot, row, to):
        values = [
            tuple(ref[i, slot, pl.ds(row, BLOCK), :].astype(jnp.float32) for i in range(2))
            for ref in sources
        ]
        for m, z in enumerate(small_dft(values, signs)):
            spec[m, slot, pl.ds(to, BLOCK), :] = z[0].astype(jnp.bfloat16)
            spec[m, slot, pl.ds(depth + to, BLOCK), :] = z[1].astype(jnp.bfloat16)

    @pl.when(step == 0)
    def _():
        acc[...] = jnp.zeros_like(acc)
        for slot in range(slots):

            @pl.loop(0, head_rows // BLOCK, unroll=2)
            def _(i):
                row = pl.multiple_of(i * BLOCK, BLOCK)
                transform(heads, slot, row, row)

            @pl.loop(0, tail_rows // BLOCK, unroll=2)
            def _(i):
                row = pl.multiple_of(i * BLOCK, BLOCK)
                transform(tails, slot, row, pl.multiple_of(head_rows + row, BLOCK))

    for j in range(together):
        m = step * together + j
        cos, sin = cos_ref[j], sin_ref[j]
        table = jnp.concatenate(
            [jnp.concatenate([cos, -sin], axis=1), jnp.concatenate([sin, cos], axis=1)], axis=0
        )
        for slot in range(0, slots, 2):
            end = min(slot + 2, slots)
            spectra = jnp.concatenate([spec[m, i] for i in range(slot, end)], axis=1)
            wave = jnp.dot(table, spectra, preferred_element_type=jnp.float32)
            lanes = slice(slot * LANES, end * LANES)
            power[j, :, lanes] = wave[:depth] * wave[:depth] + wave[depth:] * wave[depth:]

    first_row = lax.broadcasted_iota(jnp.int32, (BLOCK, LANES), 0)
    for j in range(together):

        for row in range(0, depth, BLOCK):
            rows = (first_row + row).astype(jnp.float32).astype(jnp.bfloat16)
            values = [
                power[j, row : row + BLOCK, slot * LANES : (slot + 1) * LANES]
                for slot in range(slots)
            ]
            for o, value in enumerate(five_wide(five_wide(values))):
                inside = (rows >= window_ref[j, 0, o]) & (rows < window_ref[j, 1, o])
                value = jnp.where(inside, value.astype(jnp.bfloat16), jnp.bfloat16(0))
                kept[j, o, row : row + BLOCK, :] = value

    sum_row = lax.broadcasted_iota(jnp.int32, (BLOCK, depth), 0)
    sum_col = lax.broadcasted_iota(jnp.int32, (BLOCK, depth), 1)
    for j in range(together):
        m = step * together + j
        sums = jnp.where(sum_row == 0, 1, jnp.where(sum_row == 1, count * sum_col, 0))
        sums = jnp.where(sum_row == 2, m, sums).astype(jnp.float32).astype(jnp.bfloat16)
        for o in range(0, width, 2):
            end = min(o + 2, width)
            pair = jnp.concatenate([kept[j, i] for i in range(o, end)], axis=1)
            lanes = slice(o * LANES, end * LANES)
            acc[:, lanes] += jnp.dot(sums, pair, preferred_element_type=jnp.float32)[:8]

    @pl.when(step == count // together - 1)
    def _():
        out_ref[...] = acc[...]


def window_sums(me, heads, tails, tables, windows, first_slot):
    count = len(heads)
    slots = tails[0].shape[1]
    width = 2 * REACH + slots
    together = 4
    head_rows, tail_rows = heads[0].shape[2], tails[0].shape[2]
    depth = head_rows + tail_rows
    flops = 2 * count * (2 * depth) * (2 * depth) * (slots * LANES)
    moved = 4 * tables[0].size + 16 * count * depth * LANES
    sums = pl.pallas_call(
        functools.partial(turned_kernel, count=count, slots=slots, together=together),
        grid_spec=pltpu.PrefetchScalarGridSpec(
            num_scalar_prefetch=1,
            grid=(count // together,),
            in_specs=[
                pl.BlockSpec(
                    tuple(pl.Element(n) for n in (2, slots, head_rows, LANES)),
                    lambda s, me: (0, first_slot, 0, 0),
                )
                for _ in range(count)
            ]
            + [
                pl.BlockSpec((2, slots, tail_rows, LANES), lambda s, me: (0, 0, 0, 0))
                for _ in range(count)
            ]
            + [pl.BlockSpec((together, depth, depth), lambda s, me: (s, 0, 0)) for _ in range(2)]
            + [pl.BlockSpec((together, 2, width, BLOCK, LANES), lambda s, me: (s, 0, 0, 0, 0))],
            out_specs=pl.BlockSpec((8, width * LANES), lambda s, me: (0, 0)),
            scratch_shapes=[
                pltpu.VMEM((count, slots, 2 * depth, LANES), jnp.bfloat16),
                pltpu.VMEM((together, depth, slots * LANES), jnp.float32),
                pltpu.VMEM((together, width, depth, LANES), jnp.bfloat16),
                pltpu.VMEM((8, width * LANES), jnp.float32),
            ],
        ),
        out_shape=jax.ShapeDtypeStruct((8, width * LANES), jnp.float32),
        compiler_params=pltpu.CompilerParams(vmem_limit_bytes=(12 + 5 * slots) << 20),
        cost_estimate=pl.CostEstimate(flops=flops, bytes_accessed=moved, transcendentals=0),
        name="window_sums",
    )(me, in_place(heads[0]), *heads[1:], in_place(tails[0]), *tails[1:], *tables, windows)
    return jnp.stack([sums[0], sums[1] + sums[2]]).reshape(2, width, LANES)


def wave_tables(count, depth, after):
    total = count * depth
    index = jnp.arange(depth, dtype=jnp.int32)
    index, _ = lax.optimization_barrier((index, after))
    angle = ((index[:, None] * index[None, :]) % depth).astype(jnp.float32) * (2.0 * math.pi / depth)
    turn = (jnp.arange(count, dtype=jnp.int32)[:, None] * index[None, :]).astype(jnp.float32)
    turn = turn * (2.0 * math.pi / total)
    small = (jnp.cos(angle), jnp.sin(angle), jnp.cos(turn), jnp.sin(turn))
    cos_a, sin_a, cos_b, sin_b = lax.optimization_barrier(small)
    cos_b, sin_b = cos_b[:, None, :], sin_b[:, None, :]
    cos = (cos_a * cos_b - sin_a * sin_b).astype(jnp.bfloat16)
    sin = (sin_a * cos_b + cos_a * sin_b).astype(jnp.bfloat16)
    return lax.optimization_barrier((cos, sin))


def local_fast(staves, weights, replica, start, length):
    count = lax.axis_size("band")
    blocks = lax.axis_size("ping")
    me = jnp.reshape(lax.axis_index("band"), (1,)).astype(jnp.int32)
    block = lax.axis_index("ping")
    pings, bands, bins = staves.shape[1:4]
    half = pings // PAIR
    sizes = SPLITS
    depth = bands * bins
    mine = start.shape[1]

    def send(array, r):
        return lax.ppermute(array, "band", [(i, i ^ r) for i in range(count)])

    def up(array):
        return lax.ppermute(array, "ping", [(i, i + 1) for i in range(blocks - 1)])

    def down(array):
        return lax.ppermute(array, "ping", [(i + 1, i) for i in range(blocks - 1)])

    head_bands = HEAD_STEPS * STEP_BANDS
    heads = beamform(me, staves, weights, replica, count, 0, HEAD_STEPS, STEP_BANDS, (half,))
    got_heads = [heads[0]] + [send(heads[r], r) for r in range(1, count)]

    rest = (bands - head_bands) // (2 * STEP_BANDS)
    me_next, _ = lax.optimization_barrier((me, heads[0]))
    tails = beamform(
        me_next, staves, weights, replica, count, head_bands, rest, 2 * STEP_BANDS, sizes
    )
    got_tails = []
    for i in range(len(sizes)):
        own = tails[i * count : (i + 1) * count]
        got_tails.append([own[0]] + [send(own[r], r) for r in range(1, count)])

    own_start, own_length, _ = lax.optimization_barrier((start, length, tails[0]))
    spans = jnp.stack([own_start, own_start + own_length])
    reach = half + REACH
    before = up(spans[:, pings - REACH :])
    after = down(spans[:, :REACH])
    left = jnp.concatenate([before, spans[:, :reach]], axis=1)
    right = jnp.concatenate([spans[:, pings - reach :], after], axis=1)
    windows = jnp.concatenate([left, jnp.flip(right, 1)], axis=2)
    phase = jnp.arange(count, dtype=jnp.int32)[:, None, None, None]
    windows = lax.div(windows[None] + (count - 1 - phase), count).astype(jnp.bfloat16)
    windows = jnp.broadcast_to(
        windows[:, :, :, None, :], windows.shape[:3] + (BLOCK, windows.shape[3])
    )

    tables = wave_tables(count, depth, tails[0])

    reached = half + 2 * REACH
    sums = jnp.zeros((2, reached, LANES), jnp.float32)
    slot = 0
    for i, size in enumerate(sizes):
        width = 2 * REACH + size
        near = windows[:, :, slot : slot + width]
        part = window_sums(me, got_heads, got_tails[i], tables, near, slot)
        sums = sums + jnp.pad(part, ((0, 0), (slot, reached - width - slot), (0, 0)))
        if slot < REACH <= slot + size:
            edge_left = down(sums[:, :REACH, :mine])
            edge_right = up(jnp.flip(sums[:, :REACH, mine:], 1))
        slot += size

    def unfolded(which):
        def placed(array, before):
            return jnp.pad(array, ((before, pings - before - array.shape[0]), (0, 0)))

        kept = sums[which, REACH:]
        whole = placed(kept[:, :mine], 0) + placed(jnp.flip(kept[:, mine:], 0), pings - reach)
        return whole + placed(edge_left[which], pings - REACH) + placed(edge_right[which], 0)

    weight_sum = tap_weights(block * pings, blocks * pings, pings)
    scale = (1.0 / (16.0 * count * depth)) / weight_sum[:, None]
    widths = length.astype(jnp.float32)
    total, first_moment = unfolded(0), unfolded(1)
    energy_total = total * scale
    moment = (first_moment - total * (start.astype(jnp.float32) - 0.5)) * scale
    return (moment / (widths * (energy_total + 1e-06)), energy_total / widths)


def fits(mesh, staves, weights):
    count, blocks = mesh.shape["band"], mesh.shape["ping"]
    pings, bands = staves.shape[1] // blocks, staves.shape[2] // count
    bins, depth = staves.shape[3:]
    beams = weights.shape[3]
    half = pings // PAIR
    head_bands = HEAD_STEPS * STEP_BANDS
    return (
        count == 8
        and beams * PAIR == LANES * count
        and beams % (2 * LANES) == 0
        and pings % (2 * PAIR) == 0
        and half == sum(SPLITS)
        and bins == 8
        and depth % LANES == 0
        and bands * bins % LANES == 0
        and head_bands * bins % (2 * BLOCK) == 0
        and (bands - head_bands) * bins % (2 * BLOCK) == 0
        and bands * bins <= 2 * LANES
        and bands > head_bands
        and (bands - head_bands) % (2 * STEP_BANDS) == 0
        and head_bands % (2 * STEP_BANDS) == 0
    )


def solution(mesh):
    in_specs = (
        P(None, "ping", "band", None, None),
        P(None, "band", None, None),
        P(),
        P("ping", "band"),
        P("ping", "band"),
    )
    out_specs = (P("ping", "band"), P("ping", "band"))

    def run(staves, weights, replica, start, length):
        quick = fits(mesh, staves, weights)

        def local(*arrays):
            return (local_fast if quick else local_plain)(*arrays)

        body = jax.shard_map(
            local, mesh=mesh, in_specs=in_specs, out_specs=out_specs, check_vma=False
        )
        return body(staves, weights, replica, start, length)

    return run
```

```python
import functools
import math

import jax
import jax.numpy as jnp
from jax import lax
from jax.experimental import pallas as pl
from jax.experimental.pallas import tpu as pltpu
from jax.sharding import PartitionSpec as P


TAPS = (1.0, 2.0, 3.0, 4.0, 5.0, 4.0, 3.0, 2.0, 1.0)
REACH = len(TAPS) // 2
LANES = 128
PAIR = 2
BLOCK = 16
HEAD_STEPS = 2
STEP_BANDS = 4
SPLITS = (4, 3, 1)


def extended(array, sides, width):
    for axis, dim in sides:
        count, length = (lax.axis_size(axis), array.shape[dim])
        up = [(i, (i + 1) % count) for i in range(count - 1)]
        down = [(j, i) for i, j in up]
        last = lax.slice_in_dim(array, length - width, length, axis=dim)
        initial = lax.slice_in_dim(array, 0, width, axis=dim)
        before = lax.ppermute(last, axis, up)
        after = lax.ppermute(initial, axis, down)
        array = jnp.concatenate([before, array, after], axis=dim)
    return array


def dft_tables(length_total):
    freqs = jnp.arange(length_total, dtype=jnp.int32)
    phases = freqs[:, None] * freqs[None, :] % length_total
    angles = phases.astype(jnp.float32) * (2.0 * math.pi / length_total)
    return (jnp.cos(angles).astype(jnp.bfloat16), jnp.sin(angles).astype(jnp.bfloat16))


def envelope_rows(spec_re, spec_im, replica, cos_table, sin_table):
    comp_re = (spec_re * replica[0] + spec_im * replica[1]).astype(jnp.bfloat16)
    comp_im = (spec_im * replica[0] - spec_re * replica[1]).astype(jnp.bfloat16)
    wave_re = jnp.dot(comp_re, cos_table, preferred_element_type=jnp.float32) - jnp.dot(
        comp_im, sin_table, preferred_element_type=jnp.float32
    )
    wave_im = jnp.dot(comp_re, sin_table, preferred_element_type=jnp.float32) + jnp.dot(
        comp_im, cos_table, preferred_element_type=jnp.float32
    )
    return (wave_re * wave_re + wave_im * wave_im) * (1.0 / (16.0 * cos_table.shape[0]))


def tap_weights(first_ping, total_pings, ping_count):
    positions = first_ping + jnp.arange(ping_count + 2 * REACH, dtype=jnp.int32) - REACH
    inside = ((positions >= 0) & (positions < total_pings)).astype(jnp.float32)
    weight_sum = jnp.zeros((ping_count,), jnp.float32)
    for offset, tap in enumerate(TAPS):
        weight_sum = weight_sum + tap * inside[offset : offset + ping_count]
    return weight_sum


def smooth_pings(padded, first_ping, total_pings, ping_count):
    summed = jnp.zeros((ping_count,) + padded.shape[1:], jnp.float32)
    for offset, tap in enumerate(TAPS):
        summed = summed + tap * padded[offset : offset + ping_count]
    return summed / tap_weights(first_ping, total_pings, ping_count)[:, None, None]


def window_stats(smoothed, start, length):
    samples = jnp.arange(smoothed.shape[-1], dtype=jnp.int32)
    window_start = start[..., None]
    finish = (start + length)[..., None]
    inside = (samples >= window_start) & (samples < finish)
    offsets = samples.astype(jnp.float32) - start.astype(jnp.float32)[..., None] + 0.5
    energy_total = jnp.sum(jnp.where(inside, smoothed, 0.0), axis=-1)
    moment = jnp.sum(jnp.where(inside, smoothed * offsets, 0.0), axis=-1)
    widths = length.astype(jnp.float32)
    return (moment / (widths * (energy_total + 1e-06)), energy_total / widths)


def local_plain(staves, weights, replica, start, length):
    ping_index = lax.axis_index("ping")
    ping_total = lax.axis_size("ping")
    beam_re = jnp.einsum(
        "pkfs,ksb->kpfb", staves[0], weights[0], preferred_element_type=jnp.float32
    ) - jnp.einsum("pkfs,ksb->kpfb", staves[1], weights[1], preferred_element_type=jnp.float32)
    beam_im = jnp.einsum(
        "pkfs,ksb->kpfb", staves[0], weights[1], preferred_element_type=jnp.float32
    ) + jnp.einsum("pkfs,ksb->kpfb", staves[1], weights[0], preferred_element_type=jnp.float32)
    beams = jnp.stack([beam_re, beam_im]).astype(jnp.bfloat16)
    cos_table, sin_table = dft_tables(replica.shape[1])
    turned = lax.all_to_all(beams, "band", split_axis=4, concat_axis=1, tiled=True)
    pings_here = turned.shape[2]
    beams_here = turned.shape[4]
    flat_rows = jnp.transpose(turned, (0, 2, 4, 1, 3)).reshape(2, pings_here * beams_here, -1)
    energy_rows = envelope_rows(
        flat_rows[0].astype(jnp.float32),
        flat_rows[1].astype(jnp.float32),
        replica,
        cos_table,
        sin_table,
    )
    envelope = energy_rows.reshape(pings_here, beams_here, -1)
    ping_count = envelope.shape[0]
    padded = extended(envelope.astype(jnp.bfloat16), (("ping", 0),), REACH).astype(envelope.dtype)
    smoothed = smooth_pings(padded, ping_index * ping_count, ping_total * ping_count, ping_count)
    centroid, energy = window_stats(smoothed, start, length)
    return (centroid, energy)


def beam_kernel(me_ref, x_ref, w_ref, rep_ref, *outs, count, first_band, splits):
    bands = x_ref.shape[2]
    pings, bins, staves = x_ref.shape[1], x_ref.shape[3], x_ref.shape[4]
    rows = pings * bins
    step = pl.program_id(0)
    base = (first_band + step * bands) * bins
    q_rows = lax.broadcasted_iota(jnp.int32, (bins, rep_ref.shape[1]), 0)
    q_cols = lax.broadcasted_iota(jnp.int32, (bins, rep_ref.shape[1]), 1)
    lower = lax.broadcasted_iota(jnp.int32, (2 * bins, LANES), 1) < LANES // PAIR
    swap = jnp.broadcast_to(lax.bitwise_and(me_ref[0], PAIR - 1) == 1, (2 * bins, LANES))
    places = [(i, at) for i, size in enumerate(splits) for at in range(size)]

    def spectra(k):
        def part(which):
            flat = x_ref[which, :, k].astype(jnp.float32).reshape(rows, staves)
            return flat.astype(jnp.bfloat16)

        re, im = part(0), part(1)
        both = jnp.concatenate(
            [jnp.concatenate([re, -im], axis=1), jnp.concatenate([im, re], axis=1)], axis=0
        )
        mine = q_cols == q_rows + (base + k * bins)
        rep = [
            jnp.sum(jnp.where(mine, rep_ref[i : i + 1, :], 0.0), axis=1, keepdims=True)
            for i in range(2)
        ]
        return both, rep

    def compressed(k, both, rep, groups):
        weights = jnp.concatenate(
            [
                jnp.concatenate([w_ref[which, k, :, lanes] for lanes in groups], axis=1)
                for which in range(2)
            ],
            axis=0,
        )
        beam = jnp.dot(both, weights, preferred_element_type=jnp.float32)
        beam = beam.astype(jnp.bfloat16).astype(jnp.float32)
        beam_re = beam[:rows].reshape(pings, bins, beam.shape[1])
        beam_im = beam[rows:].reshape(pings, bins, beam.shape[1])
        return (beam_re * rep[0] + beam_im * rep[1], beam_im * rep[0] - beam_re * rep[1])

    for k in range(0, bands, 2):
        pair = [spectra(k), spectra(k + 1)]
        here = slice(k * bins, (k + 2) * bins)
        for near in range(0, count, 2 * PAIR):
            groups = []
            for r in (near, near + PAIR):
                group = lax.shift_right_logical(lax.bitwise_xor(me_ref[0], r), 1)
                groups.append(pl.ds(pl.multiple_of(group * LANES, LANES), LANES))
            done = [compressed(k + i, *pair[i], groups) for i in range(2)]
            for which in range(2):
                joined = jnp.concatenate([done[0][which], done[1][which]], axis=1)
                for part in range(len(groups)):
                    lane = slice(part * LANES, (part + 1) * LANES)
                    r = near + PAIR * part
                    for slot, (i, at) in enumerate(places):
                        one, two = joined[slot, :, lane], joined[pings - 1 - slot, :, lane]
                        first = jnp.where(lower, one, pltpu.roll(two, LANES // PAIR, 1))
                        second = jnp.where(lower, pltpu.roll(one, LANES // PAIR, 1), two)
                        first, second = first.astype(jnp.bfloat16), second.astype(jnp.bfloat16)
                        outs[i * count + r][which, at, here] = jnp.where(swap, second, first)
                        outs[i * count + r + 1][which, at, here] = jnp.where(swap, first, second)


def in_place(array):
    return pltpu.with_memory_space_constraint(array, pltpu.HBM)


def beamform(me, staves, weights, replica, count, first_band, steps, bands, splits):
    pings, bins = staves.shape[1], staves.shape[3]
    depth, beams = weights.shape[2], weights.shape[3]
    local_q = weights.shape[1] * bins
    skip = first_band // bands
    rows = bands * bins
    shapes = [
        pltpu.HBM((2, size, steps * rows, LANES), jnp.bfloat16)
        for size in splits
        for _ in range(count)
    ]
    flops = 8 * steps * bands * pings * bins * depth * beams
    moved = 4 * steps * bands * depth * beams + 8 * steps * bands * pings * bins * depth
    return pl.pallas_call(
        functools.partial(beam_kernel, count=count, first_band=first_band, splits=splits),
        grid_spec=pltpu.PrefetchScalarGridSpec(
            num_scalar_prefetch=1,
            grid=(steps,),
            in_specs=[
                pl.BlockSpec((2, pings, bands, bins, depth), lambda s, me: (0, 0, skip + s, 0, 0)),
                pl.BlockSpec((2, bands, depth, beams), lambda s, me: (0, skip + s, 0, 0)),
                pl.BlockSpec((2, local_q), lambda s, me: (0, me[0])),
            ],
            out_specs=[
                pl.BlockSpec((2, size, rows, LANES), lambda s, me: (0, 0, s, 0))
                for size in splits
                for _ in range(count)
            ],
        ),
        out_shape=shapes,
        compiler_params=pltpu.CompilerParams(vmem_limit_bytes=24 << 20),
        cost_estimate=pl.CostEstimate(flops=flops, bytes_accessed=moved, transcendentals=0),
        name="beamform",
    )(me, in_place(staves), in_place(weights), in_place(replica))


def add(a, b):
    return (a[0] + b[0], a[1] + b[1])


def sub(a, b):
    return (a[0] - b[0], a[1] - b[1])


def turned(z, steps, signs, count):
    cos, sin = 1.0, 0.0
    for bit in range(steps.bit_length()):
        if steps >> bit & 1:
            angle = 2.0 * math.pi * (1 << bit) / count
            quarter = 4 << bit == count
            c, s = 0.0 if quarter else math.cos(angle), signs[bit] * math.sin(angle)
            if quarter:
                cos, sin = (-1.0 * sin * s if not isinstance(sin, float) else 0.0), cos * s
            else:
                cos, sin = c, s
    if isinstance(cos, float) and cos == 0.0:
        return (z[1] * -sin, z[0] * sin)
    return (z[0] * cos - z[1] * sin, z[1] * cos + z[0] * sin)


def small_dft(values, signs):
    count = len(values)
    if count == 1:
        return values
    middle = count // 2
    even = small_dft([add(values[i], values[i + middle]) for i in range(middle)], signs)
    apart = [sub(values[i], values[i + middle]) for i in range(middle)]
    odd = small_dft(
        [apart[0]] + [turned(apart[i], i, signs, count) for i in range(1, middle)], signs
    )
    return [even[i // 2] if i % 2 == 0 else odd[i // 2] for i in range(count)]


def five_wide(values):
    known = {}

    def run(first, size):
        if size == 1:
            return values[first]
        if (first, size) not in known:
            part = 1 << (size - 1).bit_length() - 1
            known[first, size] = run(first, part) + run(first + part, size - part)
        return known[first, size]

    count = len(values)
    ends = [(max(0, i - REACH), min(count, i + 1)) for i in range(count + REACH)]
    return [run(first, last - first) for first, last in ends]


def turned_kernel(me_ref, *refs, count, slots, together):
    heads, tails = refs[:count], refs[count : 2 * count]
    cos_ref, sin_ref, window_ref, out_ref, spec, power, kept, acc = refs[2 * count :]
    step = pl.program_id(0)
    width = 2 * REACH + slots
    head_rows, tail_rows = heads[0].shape[2], tails[0].shape[2]
    depth = head_rows + tail_rows
    signs = [
        (1 - 2 * lax.bitwise_and(lax.shift_right_logical(me_ref[0], b), 1)).astype(jnp.float32)
        for b in range(count.bit_length() - 2)
    ]

    def transform(sources, slot, row, to):
        values = [
            tuple(ref[i, slot, pl.ds(row, BLOCK), :].astype(jnp.float32) for i in range(2))
            for ref in sources
        ]
        for m, z in enumerate(small_dft(values, signs)):
            spec[m, slot, pl.ds(to, BLOCK), :] = z[0].astype(jnp.bfloat16)
            spec[m, slot, pl.ds(depth + to, BLOCK), :] = z[1].astype(jnp.bfloat16)

    @pl.when(step == 0)
    def _():
        acc[...] = jnp.zeros_like(acc)
        for slot in range(slots):

            @pl.loop(0, head_rows // BLOCK, unroll=2)
            def _(i):
                row = pl.multiple_of(i * BLOCK, BLOCK)
                transform(heads, slot, row, row)

            @pl.loop(0, tail_rows // BLOCK, unroll=2)
            def _(i):
                row = pl.multiple_of(i * BLOCK, BLOCK)
                transform(tails, slot, row, pl.multiple_of(head_rows + row, BLOCK))

    for j in range(together):
        m = step * together + j
        cos, sin = cos_ref[j], sin_ref[j]
        table = jnp.concatenate(
            [jnp.concatenate([cos, -sin], axis=1), jnp.concatenate([sin, cos], axis=1)], axis=0
        )
        for slot in range(0, slots, 2):
            end = min(slot + 2, slots)
            spectra = jnp.concatenate([spec[m, i] for i in range(slot, end)], axis=1)
            wave = jnp.dot(table, spectra, preferred_element_type=jnp.float32)
            lanes = slice(slot * LANES, end * LANES)
            power[j, :, lanes] = wave[:depth] * wave[:depth] + wave[depth:] * wave[depth:]

    first_row = lax.broadcasted_iota(jnp.int32, (BLOCK, LANES), 0)
    for j in range(together):

        for row in range(0, depth, BLOCK):
            rows = (first_row + row).astype(jnp.float32).astype(jnp.bfloat16)
            values = [
                power[j, row : row + BLOCK, slot * LANES : (slot + 1) * LANES]
                for slot in range(slots)
            ]
            for o, value in enumerate(five_wide(five_wide(values))):
                inside = (rows >= window_ref[j, 0, o]) & (rows < window_ref[j, 1, o])
                value = jnp.where(inside, value.astype(jnp.bfloat16), jnp.bfloat16(0))
                kept[j, o, row : row + BLOCK, :] = value

    sum_row = lax.broadcasted_iota(jnp.int32, (BLOCK, depth), 0)
    sum_col = lax.broadcasted_iota(jnp.int32, (BLOCK, depth), 1)
    for j in range(together):
        m = step * together + j
        sums = jnp.where(sum_row == 0, 1, jnp.where(sum_row == 1, count * sum_col, 0))
        sums = jnp.where(sum_row == 2, m, sums).astype(jnp.float32).astype(jnp.bfloat16)
        for o in range(0, width, 2):
            end = min(o + 2, width)
            pair = jnp.concatenate([kept[j, i] for i in range(o, end)], axis=1)
            lanes = slice(o * LANES, end * LANES)
            acc[:, lanes] += jnp.dot(sums, pair, preferred_element_type=jnp.float32)[:8]

    @pl.when(step == count // together - 1)
    def _():
        out_ref[...] = acc[...]


def window_sums(me, heads, tails, tables, windows, first_slot):
    count = len(heads)
    slots = tails[0].shape[1]
    width = 2 * REACH + slots
    together = 4
    head_rows, tail_rows = heads[0].shape[2], tails[0].shape[2]
    depth = head_rows + tail_rows
    flops = 2 * count * (2 * depth) * (2 * depth) * (slots * LANES)
    moved = 4 * tables[0].size + 16 * count * depth * LANES
    sums = pl.pallas_call(
        functools.partial(turned_kernel, count=count, slots=slots, together=together),
        grid_spec=pltpu.PrefetchScalarGridSpec(
            num_scalar_prefetch=1,
            grid=(count // together,),
            in_specs=[
                pl.BlockSpec(
                    tuple(pl.Element(n) for n in (2, slots, head_rows, LANES)),
                    lambda s, me: (0, first_slot, 0, 0),
                )
                for _ in range(count)
            ]
            + [
                pl.BlockSpec((2, slots, tail_rows, LANES), lambda s, me: (0, 0, 0, 0))
                for _ in range(count)
            ]
            + [pl.BlockSpec((together, depth, depth), lambda s, me: (s, 0, 0)) for _ in range(2)]
            + [pl.BlockSpec((together, 2, width, BLOCK, LANES), lambda s, me: (s, 0, 0, 0, 0))],
            out_specs=pl.BlockSpec((8, width * LANES), lambda s, me: (0, 0)),
            scratch_shapes=[
                pltpu.VMEM((count, slots, 2 * depth, LANES), jnp.bfloat16),
                pltpu.VMEM((together, depth, slots * LANES), jnp.float32),
                pltpu.VMEM((together, width, depth, LANES), jnp.bfloat16),
                pltpu.VMEM((8, width * LANES), jnp.float32),
            ],
        ),
        out_shape=jax.ShapeDtypeStruct((8, width * LANES), jnp.float32),
        compiler_params=pltpu.CompilerParams(vmem_limit_bytes=(12 + 5 * slots) << 20),
        cost_estimate=pl.CostEstimate(flops=flops, bytes_accessed=moved, transcendentals=0),
        name="window_sums",
    )(me, in_place(heads[0]), *heads[1:], in_place(tails[0]), *tails[1:], *tables, windows)
    return jnp.stack([sums[0], sums[1] + sums[2]]).reshape(2, width, LANES)


def wave_tables(count, depth, after):
    total = count * depth
    index = jnp.arange(depth, dtype=jnp.int32)
    index, _ = lax.optimization_barrier((index, after))
    angle = ((index[:, None] * index[None, :]) % depth).astype(jnp.float32) * (2.0 * math.pi / depth)
    turn = (jnp.arange(count, dtype=jnp.int32)[:, None] * index[None, :]).astype(jnp.float32)
    turn = turn * (2.0 * math.pi / total)
    small = (jnp.cos(angle), jnp.sin(angle), jnp.cos(turn), jnp.sin(turn))
    cos_a, sin_a, cos_b, sin_b = lax.optimization_barrier(small)
    cos_b, sin_b = cos_b[:, None, :], sin_b[:, None, :]
    cos = (cos_a * cos_b - sin_a * sin_b).astype(jnp.bfloat16)
    sin = (sin_a * cos_b + cos_a * sin_b).astype(jnp.bfloat16)
    return lax.optimization_barrier((cos, sin))


def local_fast(staves, weights, replica, start, length):
    count = lax.axis_size("band")
    blocks = lax.axis_size("ping")
    me = jnp.reshape(lax.axis_index("band"), (1,)).astype(jnp.int32)
    block = lax.axis_index("ping")
    pings, bands, bins = staves.shape[1:4]
    half = pings // PAIR
    sizes = SPLITS
    depth = bands * bins
    mine = start.shape[1]

    def send(array, r):
        return lax.ppermute(array, "band", [(i, i ^ r) for i in range(count)])

    def up(array):
        return lax.ppermute(array, "ping", [(i, i + 1) for i in range(blocks - 1)])

    def down(array):
        return lax.ppermute(array, "ping", [(i + 1, i) for i in range(blocks - 1)])

    head_bands = HEAD_STEPS * STEP_BANDS
    heads = beamform(me, staves, weights, replica, count, 0, HEAD_STEPS, STEP_BANDS, (half,))
    got_heads = [heads[0]] + [send(heads[r], r) for r in range(1, count)]

    rest = (bands - head_bands) // STEP_BANDS
    me_next, _ = lax.optimization_barrier((me, heads[0]))
    tails = beamform(me_next, staves, weights, replica, count, head_bands, rest, STEP_BANDS, sizes)
    got_tails = []
    for i in range(len(sizes)):
        own = tails[i * count : (i + 1) * count]
        got_tails.append([own[0]] + [send(own[r], r) for r in range(1, count)])

    own_start, own_length, _ = lax.optimization_barrier((start, length, tails[0]))
    spans = jnp.stack([own_start, own_start + own_length])
    reach = half + REACH
    before = up(spans[:, pings - REACH :])
    after = down(spans[:, :REACH])
    left = jnp.concatenate([before, spans[:, :reach]], axis=1)
    right = jnp.concatenate([spans[:, pings - reach :], after], axis=1)
    windows = jnp.concatenate([left, jnp.flip(right, 1)], axis=2)
    phase = jnp.arange(count, dtype=jnp.int32)[:, None, None, None]
    windows = lax.div(windows[None] + (count - 1 - phase), count).astype(jnp.bfloat16)
    windows = jnp.broadcast_to(
        windows[:, :, :, None, :], windows.shape[:3] + (BLOCK, windows.shape[3])
    )

    tables = wave_tables(count, depth, tails[0])

    def placed(array, before):
        return jnp.pad(array, ((before, pings - before - array.shape[0]), (0, 0)))

    def unfolded(sums, slot):
        left, right = sums[:, :mine], jnp.flip(sums[:, mine:], 0)
        return placed(left, slot) + placed(right, pings - slot - right.shape[0])

    starts = [sum(sizes[:i]) for i in range(len(sizes))]
    nears = [
        windows[:, :, slot : slot + 2 * REACH + size] for slot, size in zip(starts, sizes)
    ]
    tables, nears = lax.optimization_barrier((tables, nears))

    reached = half + 2 * REACH
    sums = jnp.zeros((2, reached, LANES), jnp.float32)
    for i, (slot, size) in enumerate(zip(starts, sizes)):
        width = 2 * REACH + size
        near = nears[i]
        if i == len(sizes) - 1:
            so_far = [
                unfolded(sums[which, REACH:], 0)
                + placed(edge_left[which], pings - REACH)
                + placed(edge_right[which], 0)
                for which in range(2)
            ]
            near, *so_far = lax.optimization_barrier((near, *so_far))
        part = window_sums(me, got_heads, got_tails[i], tables, near, slot)
        sums = sums + jnp.pad(part, ((0, 0), (slot, reached - width - slot), (0, 0)))
        if slot < REACH <= slot + size:
            edge_left = down(sums[:, :REACH, :mine])
            edge_right = up(jnp.flip(sums[:, :REACH, mine:], 1))

    total, first_moment = [
        so_far[which] + unfolded(part[which], starts[-1] - REACH) for which in range(2)
    ]

    weight_sum = tap_weights(block * pings, blocks * pings, pings)
    scale = (1.0 / (16.0 * count * depth)) / weight_sum[:, None]
    widths = length.astype(jnp.float32)
    energy_total = total * scale
    moment = (first_moment - total * (start.astype(jnp.float32) - 0.5)) * scale
    return (moment / (widths * (energy_total + 1e-06)), energy_total / widths)


def fits(mesh, staves, weights):
    count, blocks = mesh.shape["band"], mesh.shape["ping"]
    pings, bands = staves.shape[1] // blocks, staves.shape[2] // count
    bins, depth = staves.shape[3:]
    beams = weights.shape[3]
    half = pings // PAIR
    head_bands = HEAD_STEPS * STEP_BANDS
    return (
        count == 8
        and beams * PAIR == LANES * count
        and beams % (2 * LANES) == 0
        and pings % (2 * PAIR) == 0
        and half == sum(SPLITS)
        and bins == 8
        and depth % LANES == 0
        and bands * bins % LANES == 0
        and head_bands * bins % (2 * BLOCK) == 0
        and (bands - head_bands) * bins % (2 * BLOCK) == 0
        and bands * bins <= 2 * LANES
        and bands > head_bands
        and (bands - head_bands) % STEP_BANDS == 0
    )


def solution(mesh):
    in_specs = (
        P(None, "ping", "band", None, None),
        P(None, "band", None, None),
        P(),
        P("ping", "band"),
        P("ping", "band"),
    )
    out_specs = (P("ping", "band"), P("ping", "band"))

    def run(staves, weights, replica, start, length):
        quick = fits(mesh, staves, weights)

        def local(*arrays):
            return (local_fast if quick else local_plain)(*arrays)

        body = jax.shard_map(
            local, mesh=mesh, in_specs=in_specs, out_specs=out_specs, check_vma=False
        )
        return body(staves, weights, replica, start, length)

    return run
```
